256 devices in a mesh: ctx: 32 (over x, z), head: 8 (over y, core).
Axes of the slice: x: 4, y: 4, z: 8, core: 2. Of those that a mesh axis runs over, the one named last changes fastest.
Arguments:
- query_vectors: bfloat16 [12288, 4096], P('ctx', 'head'), may hold values from -6 to 6
- key_vectors: bfloat16 [12288, 4096], P('ctx', 'head'), may hold values from -11 to 11
- value_vectors: bfloat16 [12288, 4096], P('ctx', 'head'), may hold values from -6 to 6
- log_decay: float32 [12288, 4096], P('ctx', 'head'), may hold values from -0.7 to 0, as said below
- write_rate: float32 [12288, 32], P('ctx', 'head'), may hold values from 0 to 1
- out_gate: bfloat16 [12288, 4096], P('ctx', 'head'), may hold values from -6 to 6
- norm_gain: float32 [128], replicated, may hold values from 0.25 to 1.75
- out_weight: bfloat16 [4096, 2304], P('head'), may hold values from -0.09375 to 0.09375
Outputs:
- mixed: bfloat16 [12288, 2304], P(('ctx', 'head'))
The draws below stay inside these ranges and needn't reach their ends.
Inputs may be any that keep to these rules, and one draw needn't show every extreme that they name: `log_decay`: every decay lies strictly below 1.
All inputs are finite; a program needn't handle non-finite values.
Results may differ from the reference program's by a relative error of at most 0.014.
Values may be sent and summed in bfloat16 or wider, within the bound.
A program may use at most 128 MiB of HBM per device.

```python
import math
import jax
import jax.numpy as jnp
from jax import lax

D = 2304
HEAD_TOTAL = 32
HEAD_SIZE = 128
TOK_DEV = 384
TOKEN_TOTAL = 12288
HDK = 4096
N_HEAD = 8


def head_kinds(key):
    slow_share = 0.5
    return jax.random.uniform(jax.random.fold_in(key, 5), (HEAD_TOTAL,), jnp.float32) < slow_share


def draw_key_vectors(key, part):
    sequence_lanes = jax.random.split(jax.random.fold_in(key, 17), 3)
    latent_width = HEAD_SIZE // 4
    basis_signs = 2 * jax.random.randint(sequence_lanes[0], (HEAD_TOTAL, latent_width, HEAD_SIZE), 0, 2) - 1
    latent_coeffs = jax.random.randint(sequence_lanes[1], (TOKEN_TOTAL, HEAD_TOTAL, latent_width), -8, 9)
    latent_sum = jnp.einsum('tha,hac->thc', latent_coeffs, basis_signs)
    latent_part = latent_sum.astype(jnp.float32) * (1.0 / math.sqrt(24.0 * latent_width))
    own_part = jnp.clip(jax.random.normal(sequence_lanes[2], (TOKEN_TOTAL, HEAD_TOTAL, HEAD_SIZE), jnp.float32), -6.0, 6.0)
    mixed_keys = math.sqrt(0.5) * own_part + math.sqrt(0.5) * latent_part
    return mixed_keys.reshape(TOKEN_TOTAL, HEAD_TOTAL * HEAD_SIZE).astype(jnp.bfloat16)


def draw_log_decay(key, part):
    slow_heads = head_kinds(key)
    sequence_lanes = jax.random.split(jax.random.fold_in(key, 11), 6)
    fast_rates = jnp.exp(jax.random.uniform(sequence_lanes[0], (HEAD_TOTAL, HEAD_SIZE), jnp.float32, math.log(1.0 / 60.0), math.log(1.0 / 20.0)))
    gentle_rates = jax.random.uniform(sequence_lanes[1], (HEAD_TOTAL, HEAD_SIZE), jnp.float32, 0.02, 0.25) / TOKEN_TOTAL
    base_rates = jnp.where(slow_heads[:, None], gentle_rates, fast_rates).reshape(HEAD_TOTAL * HEAD_SIZE)
    block_total = TOKEN_TOTAL // TOK_DEV
    device_spread = jnp.exp(jax.random.uniform(sequence_lanes[2], (block_total, 1, HEAD_TOTAL * HEAD_SIZE), jnp.float32, math.log(0.5), math.log(2.0)))
    roughness = jax.random.uniform(sequence_lanes[3], (block_total, TOK_DEV, HEAD_TOTAL * HEAD_SIZE), jnp.float32, 0.5, 1.5)
    stable_output = (base_rates * device_spread * roughness).reshape(TOKEN_TOTAL, HEAD_TOTAL * HEAD_SIZE)
    spike_places = jax.random.randint(sequence_lanes[4], (2,), 0, TOKEN_TOTAL)
    spike_error = jax.random.uniform(sequence_lanes[5], (2, HEAD_TOTAL * HEAD_SIZE), jnp.float32, 0.22, 0.51)
    token_positions = jnp.arange(TOKEN_TOTAL)
    first_match = (token_positions == spike_places[0]).astype(jnp.float32)[:, None]
    second_match = (token_positions == spike_places[1]).astype(jnp.float32)[:, None]
    spike_events = first_match * spike_error[0][None, :] + second_match * spike_error[1][None, :]
    return -(stable_output + spike_events)


def draw_write_rate(key, part):
    slow_heads = head_kinds(key)
    sequence_lanes = jax.random.split(jax.random.fold_in(key, 13), 2)
    small_rates = jax.random.uniform(sequence_lanes[0], (TOKEN_TOTAL, HEAD_TOTAL), jnp.float32, 0.5, 2.5) * (HEAD_SIZE / (2.0 * TOKEN_TOTAL))
    large_rates = jax.random.uniform(sequence_lanes[1], (TOKEN_TOTAL, HEAD_TOTAL), jnp.float32, 0.2, 0.9)
    return jnp.where(slow_heads[None, :], small_rates, large_rates)


def block_levels(rng, dims, shards, smallest, largest):
    def one(position, parts):
        heights = jax.random.uniform(jax.random.fold_in(jax.random.fold_in(rng, 6), position), (parts,), jnp.float32, smallest / len(shards), largest / len(shards))
        return jnp.repeat(jnp.exp(heights), dims[position] // parts).reshape((-1,) + (1,) * (len(dims) - position - 1))

    factor_of = one(*shards[0])
    for cut in shards[1:]:
        factor_of = factor_of * one(*cut)
    return factor_of


def centred(stream_key, dims, width, most, pieces=(), held_as=jnp.bfloat16):
    loudness = block_levels(stream_key, dims, pieces, -0.22, 0.18) if pieces else 1.0
    values = jax.random.normal(stream_key, dims, jnp.float32) * width * loudness
    return jnp.minimum(jnp.maximum(values, -most), most).astype(held_as)


def setup_inputs(seed: int = 0) -> dict:
    seeds = jax.random.split(jax.random.key(seed), 9)
    query_vectors = centred(seeds[0], (TOKEN_TOTAL, HDK), 1.0, 6.0, ((0, 32), (1, 8)))
    key_vectors = draw_key_vectors(jax.random.fold_in(seeds[8], 71), 0)
    value_vectors = centred(seeds[2], (TOKEN_TOTAL, HDK), 1.0, 6.0, ((0, 32), (1, 8)))
    log_decay = draw_log_decay(jax.random.fold_in(seeds[8], 71), 0)
    write_rate = draw_write_rate(jax.random.fold_in(seeds[8], 71), 0)
    out_gate = centred(seeds[5], (TOKEN_TOTAL, HDK), 1.0, 6.0, ((0, 32), (1, 8)))
    norm_gain = jnp.clip(1.0 + 0.15 * jax.random.normal(seeds[6], (HEAD_SIZE,), jnp.float32), 0.25, 1.75)
    out_weight = centred(seeds[7], (HDK, D), HDK ** -0.5, 0.09375, ((0, 8),))
    return {"query_vectors": query_vectors, "key_vectors": key_vectors, "value_vectors": value_vectors, "log_decay": log_decay, "write_rate": write_rate, "out_gate": out_gate, "norm_gain": norm_gain, "out_weight": out_weight}


peak_value = lax.Precision.HIGHEST

def reference(query_vectors, key_vectors, value_vectors, log_decay, write_rate, out_gate, norm_gain, out_weight):
    queries = query_vectors.astype(jnp.float32).reshape(TOKEN_TOTAL, HEAD_TOTAL, HEAD_SIZE)
    raw_keys = key_vectors.astype(jnp.float32).reshape(TOKEN_TOTAL, HEAD_TOTAL, HEAD_SIZE)
    unit_keys = raw_keys / jnp.sqrt(lax.optimization_barrier(jnp.sum(raw_keys * raw_keys, axis=-1, keepdims=True)) + 1e-06)
    values = value_vectors.astype(jnp.float32).reshape(TOKEN_TOTAL, HEAD_TOTAL, HEAD_SIZE)
    decay_rates = jnp.exp(log_decay).reshape(TOKEN_TOTAL, HEAD_TOTAL, HEAD_SIZE)

    def token_step(state_matrix, inputs):
        query_vector_row, key_vector_row, value_row, factor, rate_now = inputs
        faded_state = state_matrix * factor[:, :, None]
        retrieved_value = jnp.einsum('rfl,rf->rl', faded_state, key_vector_row, precision=peak_value)
        update = rate_now[:, None] * (value_row - retrieved_value)
        state_matrix = faded_state + key_vector_row[:, :, None] * update[:, None, :]
        return (state_matrix, jnp.einsum('rfl,rf->rl', state_matrix, query_vector_row, precision=peak_value))
    initial = jnp.zeros((HEAD_TOTAL, HEAD_SIZE, HEAD_SIZE), jnp.float32)
    _, attended = lax.scan(token_step, initial, (queries, unit_keys, values, decay_rates, write_rate))
    mean_square = lax.optimization_barrier(jnp.mean(attended * attended, axis=-1, keepdims=True))
    gate_values = jax.nn.sigmoid(out_gate.astype(jnp.float32).reshape(TOKEN_TOTAL, HEAD_TOTAL, HEAD_SIZE))
    gated_out = attended / jnp.sqrt(mean_square + 1e-05) * norm_gain * gate_values
    gated_out = gated_out.astype(jnp.bfloat16).reshape(TOKEN_TOTAL, HEAD_TOTAL * HEAD_SIZE)
    group_width = HEAD_TOTAL // N_HEAD * HEAD_SIZE
    summed = jnp.zeros((TOKEN_TOTAL, D), jnp.float32)
    for group_index in range(N_HEAD):
        lower_col = group_index * group_width
        partial_value = jnp.dot(gated_out[:, lower_col:lower_col + group_width], out_weight[lower_col:lower_col + group_width], preferred_element_type=jnp.float32)
        summed = summed + lax.optimization_barrier(partial_value.astype(jnp.bfloat16)).astype(jnp.float32)
    return summed.astype(jnp.bfloat16)
```

```python
import jax
import jax.numpy as jnp
from jax import lax
from jax.experimental import pallas as pl
from jax.experimental.pallas import tpu as pltpu
from jax.sharding import PartitionSpec as P

HS = 128
C = 64
NX, NZ = 4, 8
NY, NC = 4, 2
MSG = 208
HALF = HS // 2
MESH = pl.DeviceIdType.MESH
bf16, f32 = jnp.bfloat16, jnp.float32
NN, NT, TN = ((1,), (0,)), ((1,), (1,)), ((0,), (0,))


def mm(a, b, dims=NN):
    return lax.dot_general(
        a.astype(bf16), b.astype(bf16), (dims, ((), ())), preferred_element_type=f32
    )


def prep_kernel(q_ref, k_ref, v_ref, ld_ref, wr_ref, qd_ref, loc_ref, msg_ref):
    h = pl.program_id(0)
    rows = q_ref.shape[0]
    n = rows // C
    kf = k_ref[...].astype(f32)
    unit = kf * lax.rsqrt(jnp.sum(kf * kf, axis=-1, keepdims=True) + 1e-6)
    wr = wr_ref[...]
    lane = lax.broadcasted_iota(jnp.int32, wr.shape, 1)
    beta = jnp.sum(jnp.where(lane == h, wr, 0.0), axis=1, keepdims=True)
    i = lax.broadcasted_iota(jnp.int32, (C, C), 0)
    j = lax.broadcasted_iota(jnp.int32, (C, C), 1)
    lower = (i >= j).astype(bf16)
    eye = (i == j).astype(f32)
    ei = lax.broadcasted_iota(jnp.int32, (HS, HS), 0)
    ej = lax.broadcasted_iota(jnp.int32, (HS, HS), 1)
    ld = ld_ref[...]
    hi = ld.astype(bf16)
    lo = (ld - hi.astype(f32)).astype(bf16)
    parts = []
    for c in range(n):
        s = slice(c * C, (c + 1) * C)
        cum = mm(lower, hi[s]) + mm(lower, lo[s])
        end = cum[C - 1 : C]
        grow = jnp.exp(cum)
        kn = beta[s] * (unit[s] * grow)
        qn = q_ref[s].astype(f32) * grow
        kb = unit[s] * jnp.exp(-cum)
        ke = unit[s] * jnp.exp(end - cum)
        ar = mm(jnp.concatenate([kn, qn], 0), kb, NT)
        coupling = jnp.where(i > j, ar[:C], 0.0)
        reading = jnp.where(i >= j, ar[C:], 0.0)
        inv = eye
        b = 1
        while b < C:
            mask = ((i // b) % 2 == 1) & ((j // b) == (i // b) - 1)
            step = jnp.where(mask, coupling, 0.0)
            inv = inv - (step if b == 1 else mm(inv, mm(step, inv)))
            b *= 2
        y = mm(inv, jnp.concatenate([kn, beta[s] * v_ref[s].astype(f32)], 1))
        ry = mm(reading, y)
        parts.append((qn - ry[:, :HS], ry[:, HS:], mm(y, ke, TN), jnp.exp(end)))
    x = jnp.concatenate([(ei == ej).astype(f32), jnp.zeros((HS, HS), f32)], 0)
    total = jnp.ones((1, HS), f32)
    for c in range(n):
        s = slice(c * C, (c + 1) * C)
        qe, rl, yk, d = parts[c]
        o = mm(qe, x, NT)
        qd_ref[s] = o[:, :HS].astype(bf16)
        loc_ref[s] = o[:, HS:] + rl
        nx = x * d - mm(x, yk[:HS])
        x = jnp.concatenate([nx[:HS], nx[HS:] + yk[HS:]], 0)
        total = total * d
    take = jnp.where(ei == ej, total, 0.0) - x[:HS]
    d1 = total.astype(bf16).astype(f32)
    d2 = (total - d1).astype(bf16).astype(f32)
    d3 = total - d1 - d2
    ti = lax.broadcasted_iota(jnp.int32, (MSG - HS - HALF, HS), 0)
    tail = jnp.where(ti == 0, d1, jnp.where(ti == 1, d2, jnp.where(ti == 2, d3, 0.0)))
    for c in range(2):
        msg_ref[c, :HS] = take.astype(bf16)
        msg_ref[c, HS : HS + HALF] = x[HS + c * HALF : HS + (c + 1) * HALF].astype(bf16)
        msg_ref[c, HS + HALF :] = tail.astype(bf16)


def mix_kernel(
    msg_ref,
    qd_ref,
    loc_ref,
    gate_ref,
    gain_ref,
    w_ref,
    out_ref,
    rmsg,
    pre,
    s0_out,
    s0_in,
    sin_out,
    sin,
    gated,
    gsib,
    weights,
    psend,
    precv,
    own,
    m_send,
    m_recv,
    x_send,
    x_recv,
    s_send,
    s_recv,
    g_send,
    g_recv,
    w_sem,
    w_send,
    w_recv,
    p_send,
    p_recv,
):
    ctx = lax.axis_index("ctx")
    head = lax.axis_index("head")
    x, z = ctx // NZ, ctx % NZ
    y, core = head // NC, head % NC
    kd = w_ref.shape[0]
    rows = qd_ref.shape[0] // (NY * NC)
    width = w_ref.shape[1]
    sib = (ctx, y * NC + (1 - core))

    def zdev(zz):
        return (x * NZ + zz, head)

    def ydev(yy):
        return (ctx, yy * NC + core)

    xnext = (lax.rem(x + 1, NX) * NZ + z, head)
    xprev = (lax.rem(x + NX - 1, NX) * NZ + z, head)
    barrier = pltpu.get_barrier_semaphore()
    peers = [zdev(lax.rem(z + s, NZ)) for s in range(1, NZ)]
    peers += [ydev(lax.rem(y + s, NY)) for s in range(1, NY)]
    peers += [sib, xnext, xprev]
    for peer in peers:
        pl.semaphore_signal(barrier, inc=1, device_id=peer, device_id_type=MESH)
    pl.semaphore_wait(barrier, len(peers))

    def remote(src, dst, send, recv, dev):
        return pltpu.make_async_remote_copy(
            src_ref=src, dst_ref=dst, send_sem=send, recv_sem=recv, device_id=dev, device_id_type=MESH
        )

    started = []
    for s in range(1, NZ):
        zz = lax.rem(z + s, NZ)
        cp = remote(msg_ref.at[zz], rmsg.at[z], m_send.at[s], m_recv.at[z], zdev(zz))
        cp.start()
        started.append(cp)
    rmsg[z] = msg_ref[z]
    wown = pltpu.make_async_copy(w_ref, weights.at[core], w_sem)
    wown.start()
    wsib = remote(w_ref, weights.at[core], w_send, w_recv, sib)
    wsib.start()

    ei = lax.broadcasted_iota(jnp.int32, (HS + HALF, HS), 0)
    ej = lax.broadcasted_iota(jnp.int32, (HS + HALF, HS), 1)
    run = (ei == ej).astype(f32)
    for zz in range(NZ):

        @pl.when(z != zz)
        def _(zz=zz):
            remote(msg_ref.at[0], rmsg.at[zz], m_send.at[0], m_recv.at[zz], zdev(zz)).wait_recv()

        pre[zz] = run
        d = jnp.sum(rmsg[zz, HS + HALF :, :].astype(f32), axis=0, keepdims=True)
        new = run * d - mm(run, rmsg[zz, :HS, :])
        run = jnp.concatenate([new[:HS], new[HS:] + rmsg[zz, HS : HS + HALF, :].astype(f32)], 0)

    chain = remote(s0_out, s0_in, x_send, x_recv, xnext)

    @pl.when(x == 0)
    def _():
        s0_in[...] = jnp.zeros_like(s0_in)

    @pl.when(x > 0)
    def _():
        remote(s0_out, s0_in, x_send, x_recv, xprev).wait_recv()

    s0 = s0_in[...]

    @pl.when(x < NX - 1)
    def _():
        s0_out[...] = mm(s0, run[:HS]) + run[HS:]
        chain.start()

    for s in range(1, NZ):
        zz = lax.rem(z + s, NZ)
        sin_out[zz] = (mm(s0, pre[zz, :HS, :]) + pre[zz, HS:, :]).astype(bf16)
        cp = remote(sin_out.at[zz], sin.at[z], s_send.at[s], s_recv.at[z], zdev(zz))
        cp.start()
        started.append(cp)
    sin[z] = (mm(s0, pre[z, :HS, :]) + pre[z, HS:, :]).astype(bf16)

    gcopies = []
    for hh in range(qd_ref.shape[1] // HS):
        for half in range(2):
            slot = 2 * hh + half

            @pl.when(z != slot)
            def _(slot=slot):
                remote(sin_out.at[0], sin.at[slot], s_send.at[0], s_recv.at[slot], zdev(slot)).wait_recv()

        state = jnp.concatenate([sin[2 * hh], sin[2 * hh + 1]], 0)
        cols = slice(hh * HS, (hh + 1) * HS)
        att = mm(qd_ref[:, cols], state, NT) + loc_ref[:, cols]
        ms = jnp.mean(att * att, axis=-1, keepdims=True)
        gate = jax.nn.sigmoid(gate_ref[:, cols].astype(f32))
        g = (att * lax.rsqrt(ms + 1e-5) * gain_ref[...] * gate).astype(bf16)
        for jj in range(NY * NC):
            gated[jj % NC, jj // NC, :, cols] = g[jj * rows : (jj + 1) * rows]
        cp = remote(
            gated.at[1 - core, :, :, cols], gsib.at[:, :, cols], g_send.at[hh], g_recv.at[hh], sib
        )
        cp.start()
        gcopies.append(cp)

    wown.wait()
    wsib.wait()
    for cp in gcopies:
        cp.wait()
    mine = gated[core].reshape(NY * rows, kd)
    other = gsib[...].reshape(NY * rows, kd)
    tile = 768
    for nt in range(width // tile):
        cols = slice(nt * tile, (nt + 1) * tile)
        acc = mm(mine, weights[core, :, cols]) + mm(other, weights[1 - core, :, cols])
        psend[:, :, cols] = acc.reshape(NY, rows, tile).astype(bf16)
        for s in (2, 1, 3):
            yy = lax.rem(y + s, NY)
            cp = remote(
                psend.at[yy, :, cols],
                precv.at[y, :, cols],
                p_send.at[s, nt],
                p_recv.at[y, nt],
                ydev(yy),
            )
            cp.start()
            started.append(cp)
    for nt in range(width // tile):
        cols = slice(nt * tile, (nt + 1) * tile)
        total = psend[y, :, cols].astype(f32)
        for s in range(1, NY):
            yy = lax.rem(y + s, NY)
            remote(
                psend.at[0, :, cols],
                precv.at[yy, :, cols],
                p_send.at[0, nt],
                p_recv.at[yy, nt],
                ydev(yy),
            ).wait_recv()
            total = total + precv[yy, :, cols].astype(f32)
        out_ref[:, cols] = total.astype(bf16)

    @pl.when(x < NX - 1)
    def _():
        chain.wait_send()

    for cp in started:
        cp.wait_send()


def on_device(q, k, v, ld, wr, gate, gain, w):
    rows, feats = q.shape
    heads = feats // HS
    blk = pl.BlockSpec((rows, HS), lambda h: (0, h))
    qd, loc, msg = pl.pallas_call(
        prep_kernel,
        grid=(heads,),
        in_specs=[blk, blk, blk, blk, pl.BlockSpec(wr.shape, lambda h: (0, 0))],
        out_specs=[blk, blk, pl.BlockSpec((2, MSG, HS), lambda h: (h, 0, 0))],
        out_shape=[
            jax.ShapeDtypeStruct((rows, feats), bf16),
            jax.ShapeDtypeStruct((rows, feats), f32),
            jax.ShapeDtypeStruct((2 * heads, MSG, HS), bf16),
        ],
        compiler_params=pltpu.CompilerParams(vmem_limit_bytes=32 << 20),
        name="prep",
    )(q, k, v, ld, wr)
    kd, width = w.shape
    rb = rows // (NY * NC)
    vm = pl.BlockSpec(memory_space=pltpu.VMEM)
    dma = pltpu.SemaphoreType.DMA
    nt = width // 768
    return pl.pallas_call(
        mix_kernel,
        in_specs=[vm, vm, vm, vm, vm, pl.BlockSpec(memory_space=pl.ANY)],
        out_specs=vm,
        out_shape=jax.ShapeDtypeStruct((rb, width), bf16),
        scratch_shapes=[
            pltpu.VMEM((NZ, MSG, HS), bf16),
            pltpu.VMEM((NZ, HS + HALF, HS), f32),
            pltpu.VMEM((HALF, HS), f32),
            pltpu.VMEM((HALF, HS), f32),
            pltpu.VMEM((NZ, HALF, HS), bf16),
            pltpu.VMEM((NZ, HALF, HS), bf16),
            pltpu.VMEM((NC, NY, rb, kd), bf16),
            pltpu.VMEM((NY, rb, kd), bf16),
            pltpu.VMEM((NC, kd, width), bf16),
            pltpu.VMEM((NY, rb, width), bf16),
            pltpu.VMEM((NY, rb, width), bf16),
            pltpu.VMEM((8, HS), f32),
            dma((NZ,)),
            dma((NZ,)),
            dma,
            dma,
            dma((NZ,)),
            dma((NZ,)),
            dma((heads,)),
            dma((heads,)),
            dma,
            dma,
            dma,
            dma((NY, nt)),
            dma((NY, nt)),
        ],
        compiler_params=pltpu.CompilerParams(
            collective_id=0, has_side_effects=True, vmem_limit_bytes=48 << 20
        ),
        name="mix",
    )(msg, qd, loc, gate, gain.reshape(1, HS), w)


def solution(mesh):
    in_specs = (
        P("ctx", "head"),
        P("ctx", "head"),
        P("ctx", "head"),
        P("ctx", "head"),
        P("ctx", "head"),
        P("ctx", "head"),
        P(),
        P("head", None),
    )
    out_specs = P(("ctx", "head"), None)
    return jax.shard_map(
        on_device, mesh=mesh, in_specs=in_specs, out_specs=out_specs, check_vma=False
    )
```

```python
import jax
import jax.numpy as jnp
from jax import lax
from jax.experimental import pallas as pl
from jax.experimental.pallas import tpu as pltpu
from jax.sharding import PartitionSpec as P

HS = 128
C = 64
W = 2 * C
NX, NZ = 4, 8
NY, NC = 4, 2
MSG = 208
HALF = HS // 2
NT_OUT = 6
MESH = pl.DeviceIdType.MESH
bf16, f32 = jnp.bfloat16, jnp.float32
NN, NT, TN = ((1,), (0,)), ((1,), (1,)), ((0,), (0,))


def mm(a, b, dims=NN):
    return lax.dot_general(
        a.astype(bf16), b.astype(bf16), (dims, ((), ())), preferred_element_type=f32
    )


def prep(heads):
    i = lax.broadcasted_iota(jnp.int32, (W, W), 0)
    j = lax.broadcasted_iota(jnp.int32, (W, W), 1)
    lower = ((i >= j) & ((i // C) == (j // C))).astype(bf16)
    eye = (i == j).astype(f32)
    zero = jnp.zeros((W, W), bf16)
    blocks = []
    for q, k, v, ld, beta in heads:
        n = q.shape[0] // W
        for p in range(n):
            s = slice(p * W, (p + 1) * W)
            blocks.append(dict(q=q[s], k=k[s], v=v[s], ld=ld[s], beta=beta[s]))
    for b in blocks:
        hi = b["ld"].astype(bf16)
        lo = (b["ld"] - hi.astype(f32)).astype(bf16)
        b["cum"] = mm(lower, hi) + mm(lower, lo)
    for b in blocks:
        kf = b["k"].astype(f32)
        unit = kf * lax.rsqrt(jnp.sum(kf * kf, axis=-1, keepdims=True) + 1e-6)
        cum = b.pop("cum")
        e1, e2 = cum[C - 1 : C], cum[W - 1 : W]
        d1, d2 = jnp.exp(e1), jnp.exp(e2)
        grow = jnp.exp(cum)
        back = (unit * jnp.exp(-cum)).astype(bf16)
        kn = b["beta"] * (unit * grow)
        qn = b["q"].astype(f32) * grow
        ke1 = unit[:C] * jnp.exp(e1 - cum[:C])
        ke2 = unit[C:] * jnp.exp(e2 - cum[C:])
        knb, qnb = kn.astype(bf16), qn.astype(bf16)
        top = mm(jnp.concatenate([knb[:C], qnb[:C]], 0), back, NT)
        earlier = jnp.concatenate([ke1.astype(bf16), back[C:]], 0)
        bot = mm(jnp.concatenate([knb[C:], qnb[C:]], 0), earlier, NT)
        b["a"] = jnp.where(i > j, jnp.concatenate([top[:C], bot[:C]], 0), 0.0).astype(bf16)
        b["r"] = jnp.where(i >= j, jnp.concatenate([top[C:], bot[C:]], 0), 0.0).astype(bf16)
        b["qn"] = jnp.concatenate([qn[:C], qn[C:] * d1], 0)
        left = jnp.concatenate([knb[:C], (kn[C:] * d1).astype(bf16)], 0)
        right = (b["beta"] * b["v"].astype(f32)).astype(bf16)
        b["rhs"] = jnp.concatenate([left, right], 1)
        b["ke"] = jnp.concatenate([(ke1 * d2).astype(bf16), ke2.astype(bf16)], 0)
        b["d"] = d1 * d2
    size = 1
    while size < W:
        mask = ((i // size) % 2 == 1) & ((j // size) == (i // size) - 1)
        for b in blocks:
            step = jnp.where(mask, b["a"], zero)
            b["st"] = step if size == 1 else mm(step, b["t"]).astype(bf16)
        for b in blocks:
            b["t"] = eye - b["st"].astype(f32) if size == 1 else b["t"] - mm(b["t"], b["st"])
        size *= 2
    for b in blocks:
        b["y"] = mm(b["t"], b["rhs"]).astype(bf16)
    for b in blocks:
        b["ry"] = mm(b["r"], b["y"])
    for b in blocks:
        b["yk"] = mm(b["y"], b["ke"], TN)
    n = len(blocks) // len(heads)
    x = [None for _ in heads]
    total = [None for _ in heads]
    qd = [[] for _ in heads]
    loc = [[] for _ in heads]
    for p in range(n):
        for h in range(len(heads)):
            b = blocks[h * n + p]
            qe = b["qn"] - b["ry"][:, :HS]
            if p == 0:
                qd[h].append(qe.astype(bf16))
                loc[h].append(b["ry"][:, HS:])
                x[h] = jnp.concatenate([eye * b["d"] - b["yk"][:HS], b["yk"][HS:]], 0)
                total[h] = b["d"]
            else:
                xb = x[h].astype(bf16)
                o = mm(qe, xb, NT)
                qd[h].append(o[:, :HS].astype(bf16))
                loc[h].append(o[:, HS:] + b["ry"][:, HS:])
                nx = x[h] * b["d"] - mm(xb, b["yk"][:HS])
                x[h] = jnp.concatenate([nx[:HS], nx[HS:] + b["yk"][HS:]], 0)
                total[h] = total[h] * b["d"]
    return [
        (qd[h], loc[h], eye * total[h] - x[h][:HS], x[h][HS:], total[h]) for h in range(len(heads))
    ]


def kernel(
    q_hbm,
    k_hbm,
    v_hbm,
    ld_hbm,
    wr_hbm,
    gate_hbm,
    gain_hbm,
    w_hbm,
    out_ref,
    q_ref,
    k_ref,
    v_ref,
    ld_ref,
    wr_ref,
    gate_ref,
    gain_ref,
    qd_ref,
    loc_ref,
    msg_ref,
    rmsg,
    pre,
    s0_out,
    s0_in,
    sin_out,
    sin,
    gated,
    gsib,
    weights,
    acc,
    psend,
    pvia,
    precv,
    in_sem,
    m_send,
    m_recv,
    x_send,
    x_recv,
    s_send,
    s_recv,
    g_send,
    g_recv,
    w_sem,
    w_send,
    w_recv,
    p_send,
    v_recv,
    p_recv,
):
    ctx = lax.axis_index("ctx")
    head = lax.axis_index("head")
    x, z = ctx // NZ, ctx % NZ
    y, core = head // NC, head % NC
    feats = qd_ref.shape[1]
    heads = feats // HS
    rows = qd_ref.shape[0] // (NY * NC)
    sib = (ctx, y * NC + (1 - core))

    def zdev(zz):
        return (x * NZ + zz, head)

    ynext = (ctx, lax.rem(y + 1, NY) * NC + core)
    yprev = (ctx, lax.rem(y + NY - 1, NY) * NC + core)
    xnext = (lax.rem(x + 1, NX) * NZ + z, head)
    xprev = (lax.rem(x + NX - 1, NX) * NZ + z, head)
    barrier = pltpu.get_barrier_semaphore()
    peers = [zdev(lax.rem(z + s, NZ)) for s in range(1, NZ)] + [ynext, yprev, sib, xnext, xprev]
    for peer in peers:
        pl.semaphore_signal(barrier, inc=1, device_id=peer, device_id_type=MESH)

    loads = []
    for n, (src, dst) in enumerate(
        (
            (ld_hbm, ld_ref),
            (k_hbm, k_ref),
            (wr_hbm, wr_ref),
            (q_hbm, q_ref),
            (v_hbm, v_ref),
            (gate_hbm, gate_ref),
            (gain_hbm, gain_ref),
        )
    ):
        cp = pltpu.make_async_copy(src, dst, in_sem.at[n])
        cp.start()
        loads.append(cp)
    wown = pltpu.make_async_copy(w_hbm, weights.at[core], w_sem)
    wown.start()
    for cp in loads:
        cp.wait()

    def remote(src, dst, send, recv, dev):
        return pltpu.make_async_remote_copy(
            src_ref=src, dst_ref=dst, send_sem=send, recv_sem=recv, device_id=dev, device_id_type=MESH
        )

    beta = wr_ref[...].T
    args = []
    for h in range(heads):
        cols = slice(h * HS, (h + 1) * HS)
        args.append((q_ref[:, cols], k_ref[:, cols], v_ref[:, cols], ld_ref[:, cols], beta[:, h : h + 1]))
    ti = lax.broadcasted_iota(jnp.int32, (MSG - HS - HALF, HS), 0)
    for h, (qd, loc, take, state, total) in enumerate(prep(args)):
        cols = slice(h * HS, (h + 1) * HS)
        for p in range(len(qd)):
            qd_ref[p * W : (p + 1) * W, cols] = qd[p]
            loc_ref[p * W : (p + 1) * W, cols] = loc[p]
        t1 = total.astype(bf16).astype(f32)
        t2 = (total - t1).astype(bf16).astype(f32)
        t3 = total - t1 - t2
        tail = jnp.where(ti == 0, t1, jnp.where(ti == 1, t2, jnp.where(ti == 2, t3, 0.0)))
        for c in range(2):
            msg_ref[2 * h + c, :HS] = take.astype(bf16)
            msg_ref[2 * h + c, HS : HS + HALF] = state[c * HALF : (c + 1) * HALF].astype(bf16)
            msg_ref[2 * h + c, HS + HALF :] = tail.astype(bf16)

    pl.semaphore_wait(barrier, len(peers))

    started = []
    for s in (4, 3, 5, 2, 6, 1, 7):
        zz = lax.rem(z + s, NZ)
        cp = remote(msg_ref.at[zz], rmsg.at[z], m_send.at[s], m_recv.at[z], zdev(zz))
        cp.start()
        started.append(cp)
    wsib = remote(w_hbm, weights.at[core], w_send, w_recv, sib)
    wsib.start()
    rmsg[z] = msg_ref[z]

    ei = lax.broadcasted_iota(jnp.int32, (HS + HALF, HS), 0)
    ej = lax.broadcasted_iota(jnp.int32, (HS + HALF, HS), 1)
    run = (ei == ej).astype(f32)
    for zz in range(NZ):

        @pl.when(z != zz)
        def _(zz=zz):
            remote(msg_ref.at[0], rmsg.at[zz], m_send.at[0], m_recv.at[zz], zdev(zz)).wait_recv()

        pre[zz] = run
        d = jnp.sum(rmsg[zz, HS + HALF :, :].astype(f32), axis=0, keepdims=True)
        new = run * d - mm(run, rmsg[zz, :HS, :])
        run = jnp.concatenate([new[:HS], new[HS:] + rmsg[zz, HS : HS + HALF, :].astype(f32)], 0)

    chain = remote(s0_out, s0_in, x_send, x_recv, xnext)

    @pl.when(x == 0)
    def _():
        s0_in[...] = jnp.zeros_like(s0_in)

    @pl.when(x > 0)
    def _():
        remote(s0_out, s0_in, x_send, x_recv, xprev).wait_recv()

    s0 = s0_in[...]

    @pl.when(x < NX - 1)
    def _():
        s0_out[...] = (mm(s0, run[:HS]) + run[HS:]).astype(bf16)
        chain.start()

    for s in (4, 3, 5, 2, 6, 1, 7):
        zz = lax.rem(z + s, NZ)
        sin_out[zz] = (mm(s0, pre[zz, :HS, :]) + pre[zz, HS:, :]).astype(bf16)
        cp = remote(sin_out.at[zz], sin.at[z], s_send.at[s], s_recv.at[z], zdev(zz))
        cp.start()
        started.append(cp)
    sin[z] = (mm(s0, pre[z, :HS, :]) + pre[z, HS:, :]).astype(bf16)

    gcopies = []
    for hh in range(heads):
        for slot in (2 * hh, 2 * hh + 1):

            @pl.when(z != slot)
            def _(slot=slot):
                remote(sin_out.at[0], sin.at[slot], s_send.at[0], s_recv.at[slot], zdev(slot)).wait_recv()

        state = jnp.concatenate([sin[2 * hh], sin[2 * hh + 1]], 0)
        cols = slice(hh * HS, (hh + 1) * HS)
        att = mm(qd_ref[:, cols], state, NT) + loc_ref[:, cols]
        ms = jnp.mean(att * att, axis=-1, keepdims=True)
        gate = jax.nn.sigmoid(gate_ref[:, cols].astype(f32))
        g = (att * lax.rsqrt(ms + 1e-5) * gain_ref[...] * gate).astype(bf16)
        for jj in range(NY * NC):
            gated[jj % NC, jj // NC, :, cols] = g[jj * rows : (jj + 1) * rows]
        cp = remote(
            gated.at[1 - core, :, :, cols], gsib.at[:, :, cols], g_send.at[hh], g_recv.at[hh], sib
        )
        cp.start()
        gcopies.append(cp)

    tile = weights.shape[2] // NT_OUT
    wown.wait()
    mine = gated[core].reshape(NY * rows, feats)
    for t in range(NT_OUT):
        acc[t] = mm(mine, weights[core, :, t * tile : (t + 1) * tile])
    wsib.wait()
    for cp in gcopies:
        cp.wait()
    other = gsib[...].reshape(NY * rows, feats)
    y1, y2, y3 = [lax.rem(y + s, NY) for s in range(1, NY)]
    order = range(NT_OUT)
    for t in order:
        val = acc[t] + mm(other, weights[1 - core, :, t * tile : (t + 1) * tile])
        psend[t] = val.reshape(NY, rows, tile).astype(bf16)
        up = t % 2 == 0
        cp = remote(psend.at[t, y2], pvia.at[t], p_send.at[0, t], v_recv.at[t], ynext if up else yprev)
        cp.start()
        started.append(cp)
        cp = remote(
            psend.at[t, y3 if up else y1],
            precv.at[1 if up else 0, t],
            p_send.at[1, t],
            p_recv.at[1 if up else 0, t],
            yprev if up else ynext,
        )
        cp.start()
        started.append(cp)
    for t in order:
        up = t % 2 == 0
        near = y1 if up else y3
        remote(
            psend.at[t, 0], pvia.at[t], p_send.at[0, t], v_recv.at[t], yprev if up else ynext
        ).wait_recv()
        psend[t, near] = (psend[t, near].astype(f32) + pvia[t].astype(f32)).astype(bf16)
        cp = remote(
            psend.at[t, near],
            precv.at[0 if up else 1, t],
            p_send.at[2, t],
            p_recv.at[0 if up else 1, t],
            ynext if up else yprev,
        )
        cp.start()
        started.append(cp)
    for t in order:
        for side in range(2):
            remote(
                psend.at[t, 0],
                precv.at[side, t],
                p_send.at[0, t],
                p_recv.at[side, t],
                yprev if side == 0 else ynext,
            ).wait_recv()
        total = psend[t, y].astype(f32) + precv[0, t].astype(f32) + precv[1, t].astype(f32)
        out_ref[:, t * tile : (t + 1) * tile] = total.astype(bf16)

    @pl.when(x < NX - 1)
    def _():
        chain.wait_send()

    for cp in started:
        cp.wait_send()


def on_device(q, k, v, ld, wr, gate, gain, w):
    toks, feats = q.shape
    heads = feats // HS
    kd, width = w.shape
    rb = toks // (NY * NC)
    tile = width // NT_OUT
    anyspec = pl.BlockSpec(memory_space=pl.ANY)
    vmem, dma = pltpu.VMEM, pltpu.SemaphoreType.DMA
    return pl.pallas_call(
        kernel,
        in_specs=[anyspec] * 8,
        out_specs=pl.BlockSpec(memory_space=pltpu.VMEM),
        out_shape=jax.ShapeDtypeStruct((rb, width), bf16),
        scratch_shapes=[
            vmem((toks, feats), bf16),
            vmem((toks, feats), bf16),
            vmem((toks, feats), bf16),
            vmem((toks, feats), f32),
            vmem((heads, toks), f32),
            vmem((toks, feats), bf16),
            vmem((1, HS), f32),
            vmem((toks, feats), bf16),
            vmem((toks, feats), f32),
            vmem((NZ, MSG, HS), bf16),
            vmem((NZ, MSG, HS), bf16),
            vmem((NZ, HS + HALF, HS), f32),
            vmem((HALF, HS), bf16),
            vmem((HALF, HS), bf16),
            vmem((NZ, HALF, HS), bf16),
            vmem((NZ, HALF, HS), bf16),
            vmem((NC, NY, rb, kd), bf16),
            vmem((NY, rb, kd), bf16),
            vmem((NC, kd, width), bf16),
            vmem((NT_OUT, NY * rb, tile), f32),
            vmem((NT_OUT, NY, rb, tile), bf16),
            vmem((NT_OUT, rb, tile), bf16),
            vmem((2, NT_OUT, rb, tile), bf16),
            dma((7,)),
            dma((NZ,)),
            dma((NZ,)),
            dma,
            dma,
            dma((NZ,)),
            dma((NZ,)),
            dma((heads,)),
            dma((heads,)),
            dma,
            dma,
            dma,
            dma((3, NT_OUT)),
            dma((NT_OUT,)),
            dma((2, NT_OUT)),
        ],
        compiler_params=pltpu.CompilerParams(
            collective_id=0, has_side_effects=True, vmem_limit_bytes=56 << 20
        ),
        name="delta_layer",
    )(q, k, v, ld, wr.T, gate, gain.reshape(1, HS), w)


def solution(mesh):
    in_specs = (
        P("ctx", "head"),
        P("ctx", "head"),
        P("ctx", "head"),
        P("ctx", "head"),
        P("ctx", "head"),
        P("ctx", "head"),
        P(),
        P("head", None),
    )
    out_specs = P(("ctx", "head"), None)
    return jax.shard_map(
        on_device, mesh=mesh, in_specs=in_specs, out_specs=out_specs, check_vma=False
    )
```

```python
import jax
import jax.numpy as jnp
from jax import lax
from jax.experimental import pallas as pl
from jax.experimental.pallas import tpu as pltpu
from jax.sharding import PartitionSpec as P

HS = 128
C = 64
W = 2 * C
NX, NZ = 4, 8
NY, NC = 4, 2
MSG = 2 * HS + 16
OWNER = (1, 5, 3, 7)
NT_OUT = 9
MESH = pl.DeviceIdType.MESH
bf16, f32 = jnp.bfloat16, jnp.float32
NN, NT, TN = ((1,), (0,)), ((1,), (1,)), ((0,), (0,))


def mm(a, b, dims=NN):
    return lax.dot_general(
        a.astype(bf16), b.astype(bf16), (dims, ((), ())), preferred_element_type=f32
    )


def prep(heads):
    i = lax.broadcasted_iota(jnp.int32, (W, W), 0)
    j = lax.broadcasted_iota(jnp.int32, (W, W), 1)
    lower = ((i >= j) & ((i // C) == (j // C))).astype(bf16)
    eye = (i == j).astype(f32)
    zero = jnp.zeros((W, W), bf16)
    blocks = []
    for q, k, v, ld, beta in heads:
        n = q.shape[0] // W
        for p in range(n):
            s = slice(p * W, (p + 1) * W)
            blocks.append(dict(q=q[s], k=k[s], v=v[s], ld=ld[s], beta=beta[s]))
    for b in blocks:
        hi = b["ld"].astype(bf16)
        lo = (b["ld"] - hi.astype(f32)).astype(bf16)
        b["cum"] = mm(lower, hi) + mm(lower, lo)
    for b in blocks:
        kf = b["k"].astype(f32)
        unit = kf * lax.rsqrt(jnp.sum(kf * kf, axis=-1, keepdims=True) + 1e-6)
        cum = b.pop("cum")
        e1, e2 = cum[C - 1 : C], cum[W - 1 : W]
        d1, d2 = jnp.exp(e1), jnp.exp(e2)
        grow = jnp.exp(cum)
        back = (unit * jnp.exp(-cum)).astype(bf16)
        kn = b["beta"] * (unit * grow)
        qn = b["q"].astype(f32) * grow
        ke1 = unit[:C] * jnp.exp(e1 - cum[:C])
        ke2 = unit[C:] * jnp.exp(e2 - cum[C:])
        knb, qnb = kn.astype(bf16), qn.astype(bf16)
        top = mm(jnp.concatenate([knb[:C], qnb[:C]], 0), back, NT)
        earlier = jnp.concatenate([ke1.astype(bf16), back[C:]], 0)
        bot = mm(jnp.concatenate([knb[C:], qnb[C:]], 0), earlier, NT)
        b["a"] = jnp.where(i > j, jnp.concatenate([top[:C], bot[:C]], 0), 0.0).astype(bf16)
        b["r"] = jnp.where(i >= j, jnp.concatenate([top[C:], bot[C:]], 0), 0.0).astype(bf16)
        b["qn"] = jnp.concatenate([qn[:C], qn[C:] * d1], 0)
        left = jnp.concatenate([knb[:C], (kn[C:] * d1).astype(bf16)], 0)
        right = (b["beta"] * b["v"].astype(f32)).astype(bf16)
        b["rhs"] = jnp.concatenate([left, right], 1)
        b["ke"] = jnp.concatenate([(ke1 * d2).astype(bf16), ke2.astype(bf16)], 0)
        b["d"] = d1 * d2
    size = 1
    while size < W:
        mask = ((i // size) % 2 == 1) & ((j // size) == (i // size) - 1)
        for b in blocks:
            step = jnp.where(mask, b["a"], zero)
            b["st"] = step if size == 1 else mm(step, b["t"]).astype(bf16)
        for b in blocks:
            b["t"] = eye - b["st"].astype(f32) if size == 1 else b["t"] - mm(b["t"], b["st"])
        size *= 2
    for b in blocks:
        b["y"] = mm(b["t"], b["rhs"]).astype(bf16)
    for b in blocks:
        b["ry"] = mm(b["r"], b["y"])
    for b in blocks:
        b["yk"] = mm(b["y"], b["ke"], TN)
    n = len(blocks) // len(heads)
    x = [None for _ in heads]
    total = [None for _ in heads]
    qd = [[] for _ in heads]
    loc = [[] for _ in heads]
    for p in range(n):
        for h in range(len(heads)):
            b = blocks[h * n + p]
            qe = b["qn"] - b["ry"][:, :HS]
            if p == 0:
                qd[h].append(qe.astype(bf16))
                loc[h].append(b["ry"][:, HS:])
                x[h] = jnp.concatenate([eye * b["d"] - b["yk"][:HS], b["yk"][HS:]], 0)
                total[h] = b["d"]
            else:
                xb = x[h].astype(bf16)
                o = mm(qe, xb, NT)
                qd[h].append(o[:, :HS].astype(bf16))
                loc[h].append(o[:, HS:] + b["ry"][:, HS:])
                nx = x[h] * b["d"] - mm(xb, b["yk"][:HS])
                x[h] = jnp.concatenate([nx[:HS], nx[HS:] + b["yk"][HS:]], 0)
                total[h] = total[h] * b["d"]
    return [
        (qd[h], loc[h], eye * total[h] - x[h][:HS], x[h][HS:], total[h]) for h in range(len(heads))
    ]


def kernel(
    q_hbm,
    k_hbm,
    v_hbm,
    ld_hbm,
    wr_hbm,
    gate_hbm,
    gain_hbm,
    w_hbm,
    out_ref,
    q_ref,
    k_ref,
    v_ref,
    ld_ref,
    wr_ref,
    gate_ref,
    gain_ref,
    qd_ref,
    loc_ref,
    msg_ref,
    rmsg,
    pre_map,
    pre_state,
    s_out,
    s_in,
    t_out,
    t_in,
    s0,
    sin_out,
    sin,
    gated,
    gsib,
    weights,
    acc,
    psend,
    pvia,
    precv,
    in_sem,
    m_send,
    m_recv,
    x_send,
    x_recv,
    s_send,
    s_recv,
    g_send,
    g_recv,
    w_sem,
    w_send,
    w_recv,
    p_send,
    v_recv,
    p_recv,
):
    ctx = lax.axis_index("ctx")
    head = lax.axis_index("head")
    x, z = ctx // NZ, ctx % NZ
    y, core = head // NC, head % NC
    feats = qd_ref.shape[2]
    heads = feats // HS
    rows = qd_ref.shape[1] // NY
    sib = (ctx, y * NC + (1 - core))

    def zdev(zz):
        return (x * NZ + zz, head)

    ynext = (ctx, lax.rem(y + 1, NY) * NC + core)
    yprev = (ctx, lax.rem(y + NY - 1, NY) * NC + core)

    def xdev(xx):
        return (xx * NZ + z, head)

    barrier = pltpu.get_barrier_semaphore()
    peers = [zdev(lax.rem(z + s, NZ)) for s in range(1, NZ)] + [ynext, yprev, sib]
    peers += [xdev(lax.rem(x + s, NX)) for s in range(1, NX)]
    for peer in peers:
        pl.semaphore_signal(barrier, inc=1, device_id=peer, device_id_type=MESH)

    loads = []
    for n, (src, dst) in enumerate(
        (
            (ld_hbm, ld_ref),
            (k_hbm, k_ref),
            (wr_hbm, wr_ref),
            (q_hbm, q_ref),
            (v_hbm, v_ref),
            (gate_hbm, gate_ref),
            (gain_hbm, gain_ref),
        )
    ):
        cp = pltpu.make_async_copy(src, dst, in_sem.at[n])
        cp.start()
        loads.append(cp)
    wown = pltpu.make_async_copy(w_hbm, weights.at[core], w_sem)
    wown.start()
    for cp in loads:
        cp.wait()

    def remote(src, dst, send, recv, dev):
        return pltpu.make_async_remote_copy(
            src_ref=src, dst_ref=dst, send_sem=send, recv_sem=recv, device_id=dev, device_id_type=MESH
        )

    beta = wr_ref[...].T
    args = []
    for h in range(heads):
        cols = slice(h * HS, (h + 1) * HS)
        args.append((q_ref[:, cols], k_ref[:, cols], v_ref[:, cols], ld_ref[:, cols], beta[:, h : h + 1]))
    ti = lax.broadcasted_iota(jnp.int32, (MSG - 2 * HS, HS), 0)
    for h, (qd, loc, take, state, total) in enumerate(prep(args)):
        cols = slice(h * HS, (h + 1) * HS)
        for p in range(len(qd)):
            lo = p * W
            while lo < (p + 1) * W:
                jj = lo // rows
                hi = min((p + 1) * W, (jj + 1) * rows)
                to = (jj // NC) * rows + lo - jj * rows
                qd_ref[jj % NC, to : to + hi - lo, cols] = qd[p][lo - p * W : hi - p * W]
                loc_ref[jj % NC, to : to + hi - lo, cols] = loc[p][lo - p * W : hi - p * W]
                lo = hi
        t1 = total.astype(bf16).astype(f32)
        t2 = (total - t1).astype(bf16).astype(f32)
        t3 = total - t1 - t2
        tail = jnp.where(ti == 0, t1, jnp.where(ti == 1, t2, jnp.where(ti == 2, t3, 0.0)))
        msg_ref[h, :HS] = take.astype(bf16)
        msg_ref[h, HS : 2 * HS] = state.astype(bf16)
        msg_ref[h, 2 * HS :] = tail.astype(bf16)

    pl.semaphore_wait(barrier, len(peers))

    sends = []
    for h in range(heads):
        sends.append(remote(msg_ref.at[h], rmsg.at[z], m_send.at[h], m_recv.at[z], zdev(OWNER[h])))

        @pl.when(z != OWNER[h])
        def _(h=h):
            sends[h].start()

        @pl.when(z == OWNER[h])
        def _(h=h):
            rmsg[OWNER[h]] = msg_ref[h]

    wsib = remote(w_hbm, weights.at[core], w_send, w_recv, sib)
    wsib.start()

    owner = z % 2 == 1
    slot = (z - 1) // 4 + 2 * (((z - 1) // 2) % 2)
    to1 = remote(s_out, s_in, x_send.at[0], x_recv.at[0], xdev(1))
    to2 = remote(s_out, s_in, x_send.at[0], x_recv.at[0], xdev(2))
    to3 = remote(s_out, s_in, x_send.at[1], x_recv.at[0], xdev(3))
    tot3 = remote(t_out, t_in, x_send.at[0], x_recv.at[1], xdev(3))
    backs = []
    for s in (4, 3, 5, 2, 6, 1, 7):
        zz = lax.rem(z + s, NZ)
        backs.append((zz, remote(sin_out.at[zz], sin.at[slot], s_send.at[s], s_recv.at[slot], zdev(zz))))

    @pl.when(owner)
    def _():
        ei = lax.broadcasted_iota(jnp.int32, (2 * HS, HS), 0)
        ej = lax.broadcasted_iota(jnp.int32, (2 * HS, HS), 1)
        run = (ei == ej).astype(f32)
        for zz in range(NZ):

            @pl.when(z != zz)
            def _(zz=zz):
                remote(msg_ref.at[0], rmsg.at[zz], m_send.at[0], m_recv.at[zz], zdev(zz)).wait_recv()

            pre_map[zz] = run[:HS].astype(bf16)
            pre_state[zz] = run[HS:]
            d = jnp.sum(rmsg[zz, 2 * HS :, :].astype(f32), axis=0, keepdims=True)
            new = run * d - mm(run, rmsg[zz, :HS, :])
            run = jnp.concatenate([new[:HS], new[HS:] + rmsg[zz, HS : 2 * HS, :].astype(f32)], 0)

        @pl.when(x == 0)
        def _():
            s_out[...] = run[HS:].astype(bf16)
            to1.start()
            s_in[...] = jnp.zeros_like(s_in)

        @pl.when(x == 2)
        def _():
            t_out[...] = run.astype(bf16)
            tot3.start()

        @pl.when(x > 0)
        def _():
            to1.wait_recv()

        @pl.when(x == 1)
        def _():
            s_out[...] = (mm(s_in[...], run[:HS]) + run[HS:]).astype(bf16)
            to3.start()
            to2.start()

        @pl.when(x < 3)
        def _():
            s0[...] = s_in[...]

        @pl.when(x == 3)
        def _():
            tot3.wait_recv()
            s0[...] = (mm(s_in[...], t_in[:HS]) + t_in[HS:].astype(f32)).astype(bf16)

        for zz, cp in backs:
            sin_out[zz] = (mm(s0[...], pre_map[zz]) + pre_state[zz]).astype(bf16)
            cp.start()
        sin[slot] = (mm(s0[...], pre_map[z]) + pre_state[z]).astype(bf16)

    for h in range(heads):

        @pl.when(z != OWNER[h])
        def _(h=h):
            remote(sin_out.at[0], sin.at[h], s_send.at[0], s_recv.at[h], zdev(OWNER[h])).wait_recv()

    gcopies = []
    for part in (1 - core, core):
        for h in range(heads):
            cols = slice(h * HS, (h + 1) * HS)
            att = mm(qd_ref[part, :, cols], sin[h], NT) + loc_ref[part, :, cols]
            ms = jnp.mean(att * att, axis=-1, keepdims=True)
            gate = jax.nn.sigmoid(gate_ref[:, part, :, cols].astype(f32).reshape(NY * rows, HS))
            g = att * lax.rsqrt(ms + 1e-5) * gain_ref[...] * gate
            gated[part, :, cols] = g.astype(bf16)
            if len(gcopies) < heads:
                cp = remote(gated.at[part, :, cols], gsib.at[:, cols], g_send.at[h], g_recv.at[h], sib)
                cp.start()
                gcopies.append(cp)

    started = []
    tile = weights.shape[2] // NT_OUT
    wown.wait()
    mine = gated[core]
    for t in range(NT_OUT):
        acc[t] = mm(mine, weights[core, :, t * tile : (t + 1) * tile])
    wsib.wait()
    for cp in gcopies:
        cp.wait()
    other = gsib[...]
    y1, y2, y3 = [lax.rem(y + s, NY) for s in range(1, NY)]
    order = range(NT_OUT)
    for t in order:
        val = acc[t] + mm(other, weights[1 - core, :, t * tile : (t + 1) * tile])
        psend[t] = val.reshape(NY, rows, tile).astype(bf16)
        up = t % 2 == 0
        cp = remote(psend.at[t, y2], pvia.at[t], p_send.at[0, t], v_recv.at[t], ynext if up else yprev)
        cp.start()
        started.append(cp)
        cp = remote(
            psend.at[t, y3 if up else y1],
            precv.at[1 if up else 0, t],
            p_send.at[1, t],
            p_recv.at[1 if up else 0, t],
            yprev if up else ynext,
        )
        cp.start()
        started.append(cp)
    for t in order:
        up = t % 2 == 0
        near = y1 if up else y3
        remote(
            psend.at[t, 0], pvia.at[t], p_send.at[0, t], v_recv.at[t], yprev if up else ynext
        ).wait_recv()
        psend[t, near] = (psend[t, near].astype(f32) + pvia[t].astype(f32)).astype(bf16)
        cp = remote(
            psend.at[t, near],
            precv.at[0 if up else 1, t],
            p_send.at[2, t],
            p_recv.at[0 if up else 1, t],
            ynext if up else yprev,
        )
        cp.start()
        started.append(cp)
    for t in order:
        for side in range(2):
            remote(
                psend.at[t, 0],
                precv.at[side, t],
                p_send.at[0, t],
                p_recv.at[side, t],
                yprev if side == 0 else ynext,
            ).wait_recv()
        total = psend[t, y].astype(f32) + precv[0, t].astype(f32) + precv[1, t].astype(f32)
        out_ref[:, t * tile : (t + 1) * tile] = total.astype(bf16)

    for h in range(heads):

        @pl.when(z != OWNER[h])
        def _(h=h):
            sends[h].wait_send()

    @pl.when(owner)
    def _():
        for _, cp in backs:
            cp.wait_send()

    @pl.when(owner & (x < 3))
    def _():
        @pl.when(x == 2)
        def _():
            tot3.wait_send()

        @pl.when(x < 2)
        def _():
            to1.wait_send()

        @pl.when(x == 1)
        def _():
            to3.wait_send()

    for cp in started:
        cp.wait_send()


def on_device(q, k, v, ld, wr, gate, gain, w):
    toks, feats = q.shape
    heads = feats // HS
    kd, width = w.shape
    rb = toks // (NY * NC)
    tile = width // NT_OUT
    anyspec = pl.BlockSpec(memory_space=pl.ANY)
    vmem, dma = pltpu.VMEM, pltpu.SemaphoreType.DMA
    return pl.pallas_call(
        kernel,
        in_specs=[anyspec] * 8,
        out_specs=pl.BlockSpec(memory_space=pltpu.VMEM),
        out_shape=jax.ShapeDtypeStruct((rb, width), bf16),
        scratch_shapes=[
            vmem((toks, feats), bf16),
            vmem((toks, feats), bf16),
            vmem((toks, feats), bf16),
            vmem((toks, feats), f32),
            vmem((heads, toks), f32),
            vmem((NY, NC, rb, feats), bf16),
            vmem((1, HS), f32),
            vmem((NC, NY * rb, feats), bf16),
            vmem((NC, NY * rb, feats), f32),
            vmem((heads, MSG, HS), bf16),
            vmem((NZ, MSG, HS), bf16),
            vmem((NZ, HS, HS), bf16),
            vmem((NZ, HS, HS), f32),
            vmem((HS, HS), bf16),
            vmem((HS, HS), bf16),
            vmem((2 * HS, HS), bf16),
            vmem((2 * HS, HS), bf16),
            vmem((HS, HS), bf16),
            vmem((NZ, HS, HS), bf16),
            vmem((heads, HS, HS), bf16),
            vmem((NC, NY * rb, kd), bf16),
            vmem((NY * rb, kd), bf16),
            vmem((NC, kd, width), bf16),
            vmem((NT_OUT, NY * rb, tile), f32),
            vmem((NT_OUT, NY, rb, tile), bf16),
            vmem((NT_OUT, rb, tile), bf16),
            vmem((2, NT_OUT, rb, tile), bf16),
            dma((7,)),
            dma((heads,)),
            dma((NZ,)),
            dma((2,)),
            dma((2,)),
            dma((NZ,)),
            dma((heads,)),
            dma((heads,)),
            dma((heads,)),
            dma,
            dma,
            dma,
            dma((3, NT_OUT)),
            dma((NT_OUT,)),
            dma((2, NT_OUT)),
        ],
        compiler_params=pltpu.CompilerParams(
            collective_id=0, has_side_effects=True, vmem_limit_bytes=56 << 20
        ),
        name="delta_layer",
    )(q, k, v, ld, wr.T, gate.reshape(NY, NC, rb, feats), gain.reshape(1, HS), w)


def solution(mesh):
    in_specs = (
        P("ctx", "head"),
        P("ctx", "head"),
        P("ctx", "head"),
        P("ctx", "head"),
        P("ctx", "head"),
        P("ctx", "head"),
        P(),
        P("head", None),
    )
    out_specs = P(("ctx", "head"), None)
    return jax.shard_map(
        on_device, mesh=mesh, in_specs=in_specs, out_specs=out_specs, check_vma=False
    )
```

```python
import jax
import jax.numpy as jnp
from jax import lax
from jax.experimental import pallas as pl
from jax.experimental.pallas import tpu as pltpu
from jax.sharding import PartitionSpec as P

HS = 128
C = 64
W = 2 * C
NX, NZ = 4, 8
NY, NC = 4, 2
MSG = 2 * HS + 16
OWNER = (1, 5, 3, 7)
NT_OUT = 6
MESH = pl.DeviceIdType.MESH
bf16, f32 = jnp.bfloat16, jnp.float32
NN, NT, TN = ((1,), (0,)), ((1,), (1,)), ((0,), (0,))


def mm(a, b, dims=NN):
    return lax.dot_general(
        a.astype(bf16), b.astype(bf16), (dims, ((), ())), preferred_element_type=f32
    )


def prep(heads):
    i = lax.broadcasted_iota(jnp.int32, (W, W), 0)
    j = lax.broadcasted_iota(jnp.int32, (W, W), 1)
    lower = ((i >= j) & ((i // C) == (j // C))).astype(bf16)
    eye = (i == j).astype(f32)
    zero = jnp.zeros((W, W), bf16)
    blocks = []
    for q, k, v, ld, beta in heads:
        n = q.shape[0] // W
        for p in range(n):
            s = slice(p * W, (p + 1) * W)
            blocks.append(dict(q=q[s], k=k[s], v=v[s], ld=ld[s], beta=beta[s]))
    for b in blocks:
        hi = b["ld"].astype(bf16)
        lo = (b["ld"] - hi.astype(f32)).astype(bf16)
        b["cum"] = mm(lower, hi) + mm(lower, lo)
    for b in blocks:
        kf = b["k"].astype(f32)
        unit = kf * lax.rsqrt(jnp.sum(kf * kf, axis=-1, keepdims=True) + 1e-6)
        cum = b.pop("cum")
        e1, e2 = cum[C - 1 : C], cum[W - 1 : W]
        d1, d2 = jnp.exp(e1), jnp.exp(e2)
        grow = jnp.exp(cum)
        back = (unit * jnp.exp(-cum)).astype(bf16)
        kn = b["beta"] * (unit * grow)
        qn = b["q"].astype(f32) * grow
        ke1 = unit[:C] * jnp.exp(e1 - cum[:C])
        ke2 = unit[C:] * jnp.exp(e2 - cum[C:])
        knb, qnb = kn.astype(bf16), qn.astype(bf16)
        top = mm(jnp.concatenate([knb[:C], qnb[:C]], 0), back, NT)
        earlier = jnp.concatenate([ke1.astype(bf16), back[C:]], 0)
        bot = mm(jnp.concatenate([knb[C:], qnb[C:]], 0), earlier, NT)
        b["a"] = jnp.where(i > j, jnp.concatenate([top[:C], bot[:C]], 0), 0.0).astype(bf16)
        b["r"] = jnp.where(i >= j, jnp.concatenate([top[C:], bot[C:]], 0), 0.0).astype(bf16)
        b["qn"] = jnp.concatenate([qn[:C], qn[C:] * d1], 0)
        left = jnp.concatenate([knb[:C], (kn[C:] * d1).astype(bf16)], 0)
        right = (b["beta"] * b["v"].astype(f32)).astype(bf16)
        b["rhs"] = jnp.concatenate([left, right], 1)
        b["ke"] = jnp.concatenate([(ke1 * d2).astype(bf16), ke2.astype(bf16)], 0)
        b["d"] = d1 * d2
    size = 1
    while size < W:
        mask = ((i // size) % 2 == 1) & ((j // size) == (i // size) - 1)
        for b in blocks:
            step = jnp.where(mask, b["a"], zero)
            b["st"] = step if size == 1 else mm(step, b["t"]).astype(bf16)
        for b in blocks:
            b["t"] = eye - b["st"].astype(f32) if size == 1 else b["t"] - mm(b["t"], b["st"])
        size *= 2
    for b in blocks:
        b["y"] = mm(b["t"], b["rhs"]).astype(bf16)
    for b in blocks:
        b["ry"] = mm(b["r"], b["y"])
    for b in blocks:
        b["yk"] = mm(b["y"], b["ke"], TN)
    n = len(blocks) // len(heads)
    x = [None for _ in heads]
    total = [None for _ in heads]
    qd = [[] for _ in heads]
    loc = [[] for _ in heads]
    for p in range(n):
        for h in range(len(heads)):
            b = blocks[h * n + p]
            qe = b["qn"] - b["ry"][:, :HS]
            if p == 0:
                qd[h].append(qe.astype(bf16))
                loc[h].append(b["ry"][:, HS:])
                x[h] = jnp.concatenate([eye * b["d"] - b["yk"][:HS], b["yk"][HS:]], 0)
                total[h] = b["d"]
            else:
                xb = x[h].astype(bf16)
                o = mm(qe, xb, NT)
                qd[h].append(o[:, :HS].astype(bf16))
                loc[h].append(o[:, HS:] + b["ry"][:, HS:])
                nx = x[h] * b["d"] - mm(xb, b["yk"][:HS])
                x[h] = jnp.concatenate([nx[:HS], nx[HS:] + b["yk"][HS:]], 0)
                total[h] = total[h] * b["d"]
    return [
        (qd[h], loc[h], eye * total[h] - x[h][:HS], x[h][HS:], total[h]) for h in range(len(heads))
    ]


def kernel(
    q_hbm,
    k_hbm,
    v_hbm,
    ld_hbm,
    wr_hbm,
    gate_hbm,
    gain_hbm,
    w_hbm,
    out_ref,
    q_ref,
    k_ref,
    v_ref,
    ld_ref,
    wr_ref,
    gate_ref,
    gain_ref,
    qd_ref,
    loc_ref,
    msg_ref,
    rmsg,
    pre_map,
    pre_state,
    s_out,
    s_in,
    t_out,
    t_in,
    s0,
    sin_out,
    sin,
    gated,
    gsib,
    weights,
    acc,
    psend,
    pvia,
    precv,
    in_sem,
    m_send,
    m_recv,
    x_send,
    x_recv,
    s_send,
    s_recv,
    g_send,
    g_recv,
    w_sem,
    w_send,
    w_recv,
    p_send,
    v_recv,
    p_recv,
):
    ctx = lax.axis_index("ctx")
    head = lax.axis_index("head")
    x, z = ctx // NZ, ctx % NZ
    y, core = head // NC, head % NC
    feats = qd_ref.shape[2]
    heads = feats // HS
    rows = qd_ref.shape[1] // NY
    sib = (ctx, y * NC + (1 - core))

    def zdev(zz):
        return (x * NZ + zz, head)

    ynext = (ctx, lax.rem(y + 1, NY) * NC + core)
    yprev = (ctx, lax.rem(y + NY - 1, NY) * NC + core)

    def xdev(xx):
        return (xx * NZ + z, head)

    barrier = pltpu.get_barrier_semaphore()
    peers = [zdev(lax.rem(z + s, NZ)) for s in range(1, NZ)] + [ynext, yprev, sib]
    peers += [xdev(lax.rem(x + s, NX)) for s in range(1, NX)]
    for peer in peers:
        pl.semaphore_signal(barrier, inc=1, device_id=peer, device_id_type=MESH)

    loads = []
    for n, (src, dst) in enumerate(
        (
            (ld_hbm, ld_ref),
            (k_hbm, k_ref),
            (wr_hbm, wr_ref),
            (q_hbm, q_ref),
            (v_hbm, v_ref),
            (gate_hbm, gate_ref),
            (gain_hbm, gain_ref),
        )
    ):
        cp = pltpu.make_async_copy(src, dst, in_sem.at[n])
        cp.start()
        loads.append(cp)
    wown = pltpu.make_async_copy(w_hbm, weights.at[core], w_sem)
    wown.start()
    for cp in loads:
        cp.wait()

    def remote(src, dst, send, recv, dev):
        return pltpu.make_async_remote_copy(
            src_ref=src, dst_ref=dst, send_sem=send, recv_sem=recv, device_id=dev, device_id_type=MESH
        )

    beta = wr_ref[...].T
    args = []
    for h in range(heads):
        cols = slice(h * HS, (h + 1) * HS)
        args.append((q_ref[:, cols], k_ref[:, cols], v_ref[:, cols], ld_ref[:, cols], beta[:, h : h + 1]))
    ti = lax.broadcasted_iota(jnp.int32, (MSG - 2 * HS, HS), 0)
    for h, (qd, loc, take, state, total) in enumerate(prep(args)):
        cols = slice(h * HS, (h + 1) * HS)
        for p in range(len(qd)):
            lo = p * W
            while lo < (p + 1) * W:
                jj = lo // rows
                hi = min((p + 1) * W, (jj + 1) * rows)
                to = (jj // NC) * rows + lo - jj * rows
                qd_ref[jj % NC, to : to + hi - lo, cols] = qd[p][lo - p * W : hi - p * W]
                loc_ref[jj % NC, to : to + hi - lo, cols] = loc[p][lo - p * W : hi - p * W]
                lo = hi
        t1 = total.astype(bf16).astype(f32)
        t2 = (total - t1).astype(bf16).astype(f32)
        t3 = total - t1 - t2
        tail = jnp.where(ti == 0, t1, jnp.where(ti == 1, t2, jnp.where(ti == 2, t3, 0.0)))
        msg_ref[h, :HS] = take.astype(bf16)
        msg_ref[h, HS : 2 * HS] = state.astype(bf16)
        msg_ref[h, 2 * HS :] = tail.astype(bf16)

    pl.semaphore_wait(barrier, len(peers))

    sends = []
    for h in range(heads):
        sends.append(remote(msg_ref.at[h], rmsg.at[z], m_send.at[h], m_recv.at[z], zdev(OWNER[h])))

        @pl.when(z != OWNER[h])
        def _(h=h):
            sends[h].start()

        @pl.when(z == OWNER[h])
        def _(h=h):
            rmsg[OWNER[h]] = msg_ref[h]

    wsib = remote(w_hbm, weights.at[core], w_send, w_recv, sib)
    wsib.start()

    owner = z % 2 == 1
    slot = (z - 1) // 4 + 2 * (((z - 1) // 2) % 2)
    states = [remote(s_out, s_in, x_send.at[xx - 1], x_recv.at[0], xdev(xx)) for xx in (3, 2, 1)]
    totals1 = [remote(t_out, t_in.at[0], x_send.at[xx - 1], x_recv.at[1], xdev(xx)) for xx in (3, 2)]
    totals2 = [remote(t_out, t_in.at[1], x_send.at[xx - 1], x_recv.at[2], xdev(xx)) for xx in (3,)]
    backs = []
    for s in (4, 3, 5, 2, 6, 1, 7):
        zz = lax.rem(z + s, NZ)
        backs.append((zz, remote(sin_out.at[zz], sin.at[slot], s_send.at[s], s_recv.at[slot], zdev(zz))))

    @pl.when(owner)
    def _():
        ei = lax.broadcasted_iota(jnp.int32, (2 * HS, HS), 0)
        ej = lax.broadcasted_iota(jnp.int32, (2 * HS, HS), 1)
        run = (ei == ej).astype(f32)
        for zz in range(NZ):

            @pl.when(z != zz)
            def _(zz=zz):
                remote(msg_ref.at[0], rmsg.at[zz], m_send.at[0], m_recv.at[zz], zdev(zz)).wait_recv()

            pre_map[zz] = run[:HS].astype(bf16)
            pre_state[zz] = run[HS:]
            d = jnp.sum(rmsg[zz, 2 * HS :, :].astype(f32), axis=0, keepdims=True)
            new = run * d - mm(run, rmsg[zz, :HS, :])
            run = jnp.concatenate([new[:HS], new[HS:] + rmsg[zz, HS : 2 * HS, :].astype(f32)], 0)

        @pl.when(x == 0)
        def _():
            s_out[...] = run[HS:].astype(bf16)
            for cp in states:
                cp.start()
            s0[...] = jnp.zeros_like(s0)

        @pl.when((x == 1) | (x == 2))
        def _():
            t_out[...] = run.astype(bf16)

        @pl.when(x == 1)
        def _():
            for cp in totals1:
                cp.start()
            states[0].wait_recv()
            s0[...] = s_in[...]

        @pl.when(x == 2)
        def _():
            totals2[0].start()

        @pl.when(x >= 2)
        def _():
            states[0].wait_recv()
            totals1[0].wait_recv()
            s0[...] = (mm(s_in[...], t_in[0, :HS]) + t_in[0, HS:].astype(f32)).astype(bf16)

        @pl.when(x == 3)
        def _():
            totals2[0].wait_recv()
            s0[...] = (mm(s0[...], t_in[1, :HS]) + t_in[1, HS:].astype(f32)).astype(bf16)

        s0v = s0[...]
        for zz in range(NZ):
            sin_out[zz] = (mm(s0v, pre_map[zz]) + pre_state[zz]).astype(bf16)
        for zz, cp in backs:
            cp.start()
        sin[slot] = sin_out[z]

    def read(part, h):
        cols = slice(h * HS, (h + 1) * HS)
        att = mm(qd_ref[part, :, cols], sin[h], NT) + loc_ref[part, :, cols]
        ms = jnp.mean(att * att, axis=-1, keepdims=True)
        gate = jax.nn.sigmoid(gate_ref[:, part, :, cols].astype(f32).reshape(NY * rows, HS))
        return (att * lax.rsqrt(ms + 1e-5) * gain_ref[...] * gate).astype(bf16)

    gcopies = []
    for pair in range(heads // 2):
        two = (2 * pair, 2 * pair + 1)
        for h in two:

            @pl.when(z != OWNER[h])
            def _(h=h):
                remote(sin_out.at[0], sin.at[h], s_send.at[0], s_recv.at[h], zdev(OWNER[h])).wait_recv()

        out = [read(1 - core, h) for h in two]
        cols = slice(two[0] * HS, (two[1] + 1) * HS)
        gated[1 - core, :, cols] = jnp.concatenate(out, 1)
        cp = remote(gated.at[1 - core, :, cols], gsib.at[:, cols], g_send.at[pair], g_recv.at[pair], sib)
        cp.start()
        gcopies.append(cp)
    for h in range(heads):
        gated[core, :, h * HS : (h + 1) * HS] = read(core, h)

    started = []
    tile = weights.shape[2] // NT_OUT
    wide = 2 * tile
    wown.wait()
    mine = gated[core]
    for t in range(NT_OUT // 2):
        acc[t] = mm(mine, weights[core, :, t * wide : (t + 1) * wide])
    wsib.wait()
    for cp in gcopies:
        cp.wait()
    other = gsib[...]
    y1, y2, y3 = [lax.rem(y + s, NY) for s in range(1, NY)]
    for t in range(NT_OUT // 2):
        val = acc[t] + mm(other, weights[1 - core, :, t * wide : (t + 1) * wide])
        val = val.reshape(NY, rows, wide).astype(bf16)
        for u in range(2):
            psend[2 * t + u] = val[:, :, u * tile : (u + 1) * tile]
        for u in range(2):
            n = 2 * t + u
            cp = remote(psend.at[n, y2], pvia.at[n], p_send.at[0, n], v_recv.at[n], (ynext, yprev)[u])
            cp.start()
            started.append(cp)
    for t in range(NT_OUT):
        u = t % 2
        cp = remote(
            psend.at[t, (y3, y1)[u]],
            precv.at[1 - u, t],
            p_send.at[1, t],
            p_recv.at[1 - u, t],
            (yprev, ynext)[u],
        )
        cp.start()
        started.append(cp)
    for t in range(NT_OUT // 2):
        for u in range(2):
            n = 2 * t + u
            remote(
                psend.at[n, 0], pvia.at[n], p_send.at[0, n], v_recv.at[n], (yprev, ynext)[u]
            ).wait_recv()
        for u in range(2):
            n = 2 * t + u
            near = (y1, y3)[u]
            psend[n, near] = (psend[n, near].astype(f32) + pvia[n].astype(f32)).astype(bf16)
        for u in range(2):
            n = 2 * t + u
            cp = remote(
                psend.at[n, (y1, y3)[u]],
                precv.at[u, n],
                p_send.at[2, n],
                p_recv.at[u, n],
                (ynext, yprev)[u],
            )
            cp.start()
            started.append(cp)
    for t in range(NT_OUT):
        for side in range(2):
            remote(
                psend.at[t, 0],
                precv.at[side, t],
                p_send.at[0, t],
                p_recv.at[side, t],
                (yprev, ynext)[side],
            ).wait_recv()
        total = psend[t, y].astype(f32) + precv[0, t].astype(f32) + precv[1, t].astype(f32)
        out_ref[:, t * tile : (t + 1) * tile] = total.astype(bf16)

    for h in range(heads):

        @pl.when(z != OWNER[h])
        def _(h=h):
            sends[h].wait_send()

    @pl.when(owner)
    def _():
        for _, cp in backs:
            cp.wait_send()

    for xx, copies in enumerate((states, totals1, totals2)):

        @pl.when(owner & (x == xx))
        def _(copies=copies):
            for cp in copies:
                cp.wait_send()

    for cp in started:
        cp.wait_send()


def on_device(q, k, v, ld, wr, gate, gain, w):
    toks, feats = q.shape
    heads = feats // HS
    kd, width = w.shape
    rb = toks // (NY * NC)
    tile = width // NT_OUT
    anyspec = pl.BlockSpec(memory_space=pl.ANY)
    vmem, dma = pltpu.VMEM, pltpu.SemaphoreType.DMA
    return pl.pallas_call(
        kernel,
        in_specs=[anyspec] * 8,
        out_specs=pl.BlockSpec(memory_space=pltpu.VMEM),
        out_shape=jax.ShapeDtypeStruct((rb, width), bf16),
        scratch_shapes=[
            vmem((toks, feats), bf16),
            vmem((toks, feats), bf16),
            vmem((toks, feats), bf16),
            vmem((toks, feats), f32),
            vmem((heads, toks), f32),
            vmem((NY, NC, rb, feats), bf16),
            vmem((1, HS), f32),
            vmem((NC, NY * rb, feats), bf16),
            vmem((NC, NY * rb, feats), f32),
            vmem((heads, MSG, HS), bf16),
            vmem((NZ, MSG, HS), bf16),
            vmem((NZ, HS, HS), bf16),
            vmem((NZ, HS, HS), f32),
            vmem((HS, HS), bf16),
            vmem((HS, HS), bf16),
            vmem((2 * HS, HS), bf16),
            vmem((2, 2 * HS, HS), bf16),
            vmem((HS, HS), bf16),
            vmem((NZ, HS, HS), bf16),
            vmem((heads, HS, HS), bf16),
            vmem((NC, NY * rb, kd), bf16),
            vmem((NY * rb, kd), bf16),
            vmem((NC, kd, width), bf16),
            vmem((NT_OUT // 2, NY * rb, 2 * tile), f32),
            vmem((NT_OUT, NY, rb, tile), bf16),
            vmem((NT_OUT, rb, tile), bf16),
            vmem((2, NT_OUT, rb, tile), bf16),
            dma((7,)),
            dma((heads,)),
            dma((NZ,)),
            dma((3,)),
            dma((3,)),
            dma((NZ,)),
            dma((heads,)),
            dma((heads,)),
            dma((heads,)),
            dma,
            dma,
            dma,
            dma((3, NT_OUT)),
            dma((NT_OUT,)),
            dma((2, NT_OUT)),
        ],
        compiler_params=pltpu.CompilerParams(
            collective_id=0, has_side_effects=True, vmem_limit_bytes=56 << 20
        ),
        name="delta_layer",
    )(q, k, v, ld, wr.T, gate.reshape(NY, NC, rb, feats), gain.reshape(1, HS), w)


def solution(mesh):
    in_specs = (
        P("ctx", "head"),
        P("ctx", "head"),
        P("ctx", "head"),
        P("ctx", "head"),
        P("ctx", "head"),
        P("ctx", "head"),
        P(),
        P("head", None),
    )
    out_specs = P(("ctx", "head"), None)
    return jax.shard_map(
        on_device, mesh=mesh, in_specs=in_specs, out_specs=out_specs, check_vma=False
    )
```

```python
import jax
import jax.numpy as jnp
from jax import lax
from jax.experimental import pallas as pl
from jax.experimental.pallas import tpu as pltpu
from jax.sharding import PartitionSpec as P

HS = 128
C = 64
W = 2 * C
NX, NZ = 4, 8
NY, NC = 4, 2
MSG = 2 * HS + 16
OWNER = (0, 4, 2, 6)
NT_OUT = 6
MESH = pl.DeviceIdType.MESH
bf16, f32 = jnp.bfloat16, jnp.float32
NN, NT, TN = ((1,), (0,)), ((1,), (1,)), ((0,), (0,))


def mm(a, b, dims=NN):
    return lax.dot_general(
        a.astype(bf16), b.astype(bf16), (dims, ((), ())), preferred_element_type=f32
    )


def masks():
    i = lax.broadcasted_iota(jnp.int32, (W, W), 0)
    j = lax.broadcasted_iota(jnp.int32, (W, W), 1)
    return i, j


def prep_maps(n_heads, n_blocks, read):
    i, j = masks()
    lower = ((i >= j) & ((i // C) == (j // C))).astype(bf16)
    eye = (i == j).astype(f32)
    zero = jnp.zeros((W, W), bf16)
    blocks = [dict(h=h, p=p) for h in range(n_heads) for p in range(n_blocks)]
    for b in blocks:
        ld = read("ld", b)
        hi = ld.astype(bf16)
        lo = (ld - hi.astype(f32)).astype(bf16)
        b["cum"] = mm(lower, hi) + mm(lower, lo)
    for b in blocks:
        kf = read("k", b).astype(f32)
        unit = kf * lax.rsqrt(jnp.sum(kf * kf, axis=-1, keepdims=True) + 1e-6)
        cum = b.pop("cum")
        b["beta"] = read("beta", b)
        e1, e2 = cum[C - 1 : C], cum[W - 1 : W]
        d1, d2 = jnp.exp(e1), jnp.exp(e2)
        grow = jnp.exp(cum)
        back = (unit * jnp.exp(-cum)).astype(bf16)
        kn = b["beta"] * (unit * grow)
        ke1 = unit[:C] * jnp.exp(e1 - cum[:C])
        ke2 = unit[C:] * jnp.exp(e2 - cum[C:])
        knb = kn.astype(bf16)
        earlier = jnp.concatenate([ke1.astype(bf16), back[C:]], 0)
        a = jnp.concatenate([mm(knb[:C], back, NT), mm(knb[C:], earlier, NT)], 0)
        b["a"] = jnp.where(i > j, a, 0.0).astype(bf16)
        b["left"] = jnp.concatenate([knb[:C], (kn[C:] * d1).astype(bf16)], 0)
        b["ke"] = jnp.concatenate([(ke1 * d2).astype(bf16), ke2.astype(bf16)], 0)
        b["d"] = d1 * d2
        b["later"] = (grow, d1, back, earlier)
    size = 1
    while size < W:
        mask = ((i // size) % 2 == 1) & ((j // size) == (i // size) - 1)
        for b in blocks:
            step = jnp.where(mask, b["a"], zero)
            b["st"] = step if size == 1 else mm(step, b["t"]).astype(bf16)
        for b in blocks:
            b["t"] = eye - b["st"].astype(f32) if size == 1 else b["t"] - mm(b["t"], b["st"])
        size *= 2
    for b in blocks:
        right = (b["beta"] * read("v", b).astype(f32)).astype(bf16)
        b["y"] = mm(b["t"], jnp.concatenate([b["left"], right], 1)).astype(bf16)
    for b in blocks:
        b["yk"] = mm(b["y"], b["ke"], TN)
    x = [None] * n_heads
    total = [None] * n_heads
    for p in range(n_blocks):
        for h in range(n_heads):
            b = blocks[h * n_blocks + p]
            if p == 0:
                x[h] = jnp.concatenate([eye * b["d"] - b["yk"][:HS], b["yk"][HS:]], 0)
                total[h] = b["d"]
            else:
                b["x"] = x[h].astype(bf16)
                nx = x[h] * b["d"] - mm(b["x"], b["yk"][:HS])
                x[h] = jnp.concatenate([nx[:HS], nx[HS:] + b["yk"][HS:]], 0)
                total[h] = total[h] * b["d"]
    ends = [(eye * total[h] - x[h][:HS], x[h][HS:], total[h]) for h in range(n_heads)]
    return blocks, ends


def prep_reads(blocks, read, write):
    i, j = masks()
    for b in blocks:
        grow, d1, back, earlier = b["later"]
        qn = read("q", b).astype(f32) * grow
        qnb = qn.astype(bf16)
        r = jnp.concatenate([mm(qnb[:C], back, NT), mm(qnb[C:], earlier, NT)], 0)
        b["r"] = jnp.where(i >= j, r, 0.0).astype(bf16)
        b["qn"] = jnp.concatenate([qn[:C], qn[C:] * d1], 0)
    for b in blocks:
        b["ry"] = mm(b["r"], b["y"])
    for b in blocks:
        qe, local = b["qn"] - b["ry"][:, :HS], b["ry"][:, HS:]
        if "x" in b:
            o = mm(qe, b["x"], NT)
            qe, local = o[:, :HS], o[:, HS:] + local
        write(b, qe.astype(bf16), local)


def kernel(
    q_hbm,
    k_hbm,
    v_hbm,
    ld_hbm,
    wr_hbm,
    gate_hbm,
    gain_hbm,
    w_hbm,
    own_hbm,
    prev_hbm,
    next_hbm,
    q_ref,
    k_ref,
    v_ref,
    ld_ref,
    wr_ref,
    gate_ref,
    gain_ref,
    qd_ref,
    loc_ref,
    msg_ref,
    rmsg,
    pre_map,
    pre_state,
    s_out,
    s_in,
    t_out,
    t_in,
    s0,
    sin_out,
    sin,
    gated,
    gsib,
    weights,
    acc,
    psend,
    pvia,
    in_sem,
    m_send,
    m_recv,
    x_send,
    x_recv,
    s_send,
    s_recv,
    g_send,
    g_recv,
    w_sem,
    w_send,
    w_recv,
    p_send,
    v_recv,
    p_recv,
    o_sem,
):
    outs = (prev_hbm, next_hbm)
    ctx = lax.axis_index("ctx")
    head = lax.axis_index("head")
    x, z = ctx // NZ, ctx % NZ
    y, core = head // NC, head % NC
    feats = qd_ref.shape[2]
    heads = feats // HS
    rows = qd_ref.shape[1] // NY
    sib = (ctx, y * NC + (1 - core))

    def zdev(zz):
        return (x * NZ + zz, head)

    ynext = (ctx, lax.rem(y + 1, NY) * NC + core)
    yprev = (ctx, lax.rem(y + NY - 1, NY) * NC + core)

    def xdev(xx):
        return (xx * NZ + z, head)

    barrier = pltpu.get_barrier_semaphore()
    peers = [zdev(lax.rem(z + s, NZ)) for s in range(1, NZ)] + [ynext, yprev, sib]
    peers += [xdev(lax.rem(x + s, NX)) for s in range(1, NX)]
    for peer in peers:
        pl.semaphore_signal(barrier, inc=1, device_id=peer, device_id_type=MESH)

    loads = []
    for n, (src, dst) in enumerate(
        (
            (ld_hbm, ld_ref),
            (k_hbm, k_ref),
            (wr_hbm, wr_ref),
            (v_hbm, v_ref),
            (q_hbm, q_ref),
            (gate_hbm, gate_ref),
            (gain_hbm, gain_ref),
        )
    ):
        cp = pltpu.make_async_copy(src, dst, in_sem.at[n])
        cp.start()
        loads.append(cp)
    wown = pltpu.make_async_copy(w_hbm, weights.at[core], w_sem)
    wown.start()

    def remote(src, dst, send, recv, dev):
        return pltpu.make_async_remote_copy(
            src_ref=src, dst_ref=dst, send_sem=send, recv_sem=recv, device_id=dev, device_id_type=MESH
        )

    waited = set()

    def read(name, b):
        for n in dict(ld=(0,), k=(1,), beta=(2,), v=(3,), q=(4,))[name]:
            if n not in waited:
                waited.add(n)
                loads[n].wait()
        at = (slice(b["p"] * W, (b["p"] + 1) * W), slice(b["h"] * HS, (b["h"] + 1) * HS))
        if name == "beta":
            if "beta" not in cache:
                cache["beta"] = wr_ref[...].T
            return cache["beta"][at[0], b["h"] : b["h"] + 1]
        return dict(ld=ld_ref, k=k_ref, v=v_ref, q=q_ref)[name][at]

    cache = {}
    ti = lax.broadcasted_iota(jnp.int32, (MSG - 2 * HS, HS), 0)
    blocks, ends = prep_maps(heads, q_ref.shape[0] // W, read)
    for h, (take, state, total) in enumerate(ends):
        t1 = total.astype(bf16).astype(f32)
        t2 = (total - t1).astype(bf16).astype(f32)
        t3 = total - t1 - t2
        tail = jnp.where(ti == 0, t1, jnp.where(ti == 1, t2, jnp.where(ti == 2, t3, 0.0)))
        msg_ref[h, :HS] = take.astype(bf16)
        msg_ref[h, HS : 2 * HS] = state.astype(bf16)
        msg_ref[h, 2 * HS :] = tail.astype(bf16)

    pl.semaphore_wait(barrier, len(peers))

    sends = []
    for h in range(heads):
        sends.append(remote(msg_ref.at[h], rmsg.at[z], m_send.at[h], m_recv.at[z], zdev(OWNER[h] + core)))

        @pl.when(z != OWNER[h] + core)
        def _(h=h):
            sends[h].start()

        @pl.when(z == OWNER[h] + core)
        def _(h=h):
            rmsg[z] = msg_ref[h]

    wsib = remote(w_hbm, weights.at[core], w_send, w_recv, sib)
    wsib.start()

    owner = z % 2 == core
    slot = (z // 4) + 2 * ((z // 2) % 2)

    def write(b, qd, local):
        cols = slice(b["h"] * HS, (b["h"] + 1) * HS)
        lo = b["p"] * W
        while lo < (b["p"] + 1) * W:
            jj = lo // rows
            hi = min((b["p"] + 1) * W, (jj + 1) * rows)
            to = (jj // NC) * rows + lo - jj * rows
            qd_ref[jj % NC, to : to + hi - lo, cols] = qd[lo - b["p"] * W : hi - b["p"] * W]
            loc_ref[jj % NC, to : to + hi - lo, cols] = local[lo - b["p"] * W : hi - b["p"] * W]
            lo = hi

    prep_reads(blocks, read, write)
    for n in (5, 6):
        loads[n].wait()
    states = [remote(s_out, s_in, x_send.at[xx - 1], x_recv.at[0], xdev(xx)) for xx in (3, 2, 1)]
    totals1 = [remote(t_out, t_in.at[0], x_send.at[xx - 1], x_recv.at[1], xdev(xx)) for xx in (3, 2)]
    totals2 = [remote(t_out, t_in.at[1], x_send.at[xx - 1], x_recv.at[2], xdev(xx)) for xx in (3,)]
    backs = []
    for s in (4, 3, 5, 2, 6, 1, 7):
        zz = lax.rem(z + s, NZ)
        backs.append((zz, remote(sin_out.at[zz], sin.at[slot], s_send.at[s], s_recv.at[slot], zdev(zz))))

    @pl.when(owner)
    def _():
        ei = lax.broadcasted_iota(jnp.int32, (2 * HS, HS), 0)
        ej = lax.broadcasted_iota(jnp.int32, (2 * HS, HS), 1)
        run = (ei == ej).astype(f32)
        for zz in range(NZ):

            @pl.when(z != zz)
            def _(zz=zz):
                remote(msg_ref.at[0], rmsg.at[zz], m_send.at[0], m_recv.at[zz], zdev(zz)).wait_recv()

            pre_map[zz] = run[:HS].astype(bf16)
            pre_state[zz] = run[HS:]
            d = jnp.sum(rmsg[zz, 2 * HS :, :].astype(f32), axis=0, keepdims=True)
            new = run * d - mm(run, rmsg[zz, :HS, :])
            run = jnp.concatenate([new[:HS], new[HS:] + rmsg[zz, HS : 2 * HS, :].astype(f32)], 0)

        @pl.when(x == 0)
        def _():
            s_out[...] = run[HS:].astype(bf16)
            for cp in states:
                cp.start()
            s0[...] = jnp.zeros_like(s0)

        @pl.when((x == 1) | (x == 2))
        def _():
            t_out[...] = run.astype(bf16)

        @pl.when(x == 1)
        def _():
            for cp in totals1:
                cp.start()
            states[0].wait_recv()
            s0[...] = s_in[...]

        @pl.when(x == 2)
        def _():
            totals2[0].start()

        @pl.when(x >= 2)
        def _():
            states[0].wait_recv()
            totals1[0].wait_recv()
            s0[...] = (mm(s_in[...], t_in[0, :HS]) + t_in[0, HS:].astype(f32)).astype(bf16)

        @pl.when(x == 3)
        def _():
            totals2[0].wait_recv()
            s0[...] = (mm(s0[...], t_in[1, :HS]) + t_in[1, HS:].astype(f32)).astype(bf16)

        s0v = s0[...]
        for zz in range(NZ):
            sin_out[zz] = (mm(s0v, pre_map[zz]) + pre_state[zz]).astype(bf16)
        for zz, cp in backs:
            cp.start()
        sin[slot] = sin_out[z]

    def read(part, h):
        cols = slice(h * HS, (h + 1) * HS)
        att = mm(qd_ref[part, :, cols], sin[h], NT) + loc_ref[part, :, cols]
        ms = jnp.mean(att * att, axis=-1, keepdims=True)
        gate = jax.nn.sigmoid(gate_ref[:, part, :, cols].astype(f32).reshape(NY * rows, HS))
        return (att * lax.rsqrt(ms + 1e-5) * gain_ref[...] * gate).astype(bf16)

    gcopies = []
    for pair in range(heads // 2):
        two = (2 * pair, 2 * pair + 1)
        for h in two:

            @pl.when(z != OWNER[h] + core)
            def _(h=h):
                remote(sin_out.at[0], sin.at[h], s_send.at[0], s_recv.at[h], zdev(OWNER[h] + core)).wait_recv()

        out = [read(1 - core, h) for h in two]
        cols = slice(two[0] * HS, (two[1] + 1) * HS)
        gated[1 - core, :, cols] = jnp.concatenate(out, 1)
        cp = remote(gated.at[1 - core, :, cols], gsib.at[:, cols], g_send.at[pair], g_recv.at[pair], sib)
        cp.start()
        gcopies.append(cp)
    for h in range(heads):
        gated[core, :, h * HS : (h + 1) * HS] = read(core, h)

    started = []
    tile = weights.shape[2] // NT_OUT
    wide = 2 * tile
    wown.wait()
    mine = gated[core]
    for t in range(NT_OUT // 2):
        acc[t] = mm(mine, weights[core, :, t * wide : (t + 1) * wide])
    wsib.wait()
    for cp in gcopies:
        cp.wait()
    other = gsib[...]
    y1, y2, y3 = [lax.rem(y + s, NY) for s in range(1, NY)]
    for t in range(NT_OUT // 2):
        val = acc[t] + mm(other, weights[1 - core, :, t * wide : (t + 1) * wide])
        val = val.reshape(NY, rows, wide).astype(bf16)
        for u in range(2):
            psend[2 * t + u] = val[:, :, u * tile : (u + 1) * tile]
        for u in range(2):
            n = 2 * t + u
            cp = remote(psend.at[n, y2], pvia.at[n], p_send.at[0, n], v_recv.at[n], (ynext, yprev)[u])
            cp.start()
            started.append(cp)
    for t in range(NT_OUT):
        u = t % 2
        cp = remote(
            psend.at[t, (y3, y1)[u]],
            outs[1 - u].at[:, t * tile : (t + 1) * tile],
            p_send.at[1, t],
            p_recv.at[1 - u, t],
            (yprev, ynext)[u],
        )
        cp.start()
        started.append(cp)
    locals_ = []
    for t in range(NT_OUT):
        cp = pltpu.make_async_copy(psend.at[t, y], own_hbm.at[:, t * tile : (t + 1) * tile], o_sem.at[t])
        cp.start()
        locals_.append(cp)
    for t in range(NT_OUT // 2):
        for u in range(2):
            n = 2 * t + u
            remote(
                psend.at[n, 0], pvia.at[n], p_send.at[0, n], v_recv.at[n], (yprev, ynext)[u]
            ).wait_recv()
        for u in range(2):
            n = 2 * t + u
            near = (y1, y3)[u]
            psend[n, near] = (psend[n, near].astype(f32) + pvia[n].astype(f32)).astype(bf16)
        for u in range(2):
            n = 2 * t + u
            cp = remote(
                psend.at[n, (y1, y3)[u]],
                outs[u].at[:, n * tile : (n + 1) * tile],
                p_send.at[2, n],
                p_recv.at[u, n],
                (ynext, yprev)[u],
            )
            cp.start()
            started.append(cp)
    for t in range(NT_OUT):
        for side in range(2):
            cols = slice(t * tile, (t + 1) * tile)
            remote(
                psend.at[t, 0], outs[side].at[:, cols], p_send.at[0, t], p_recv.at[side, t], (yprev, ynext)[side]
            ).wait_recv()
    for cp in locals_:
        cp.wait()

    for h in range(heads):

        @pl.when(z != OWNER[h] + core)
        def _(h=h):
            sends[h].wait_send()

    @pl.when(owner)
    def _():
        for _, cp in backs:
            cp.wait_send()

    for xx, copies in enumerate((states, totals1, totals2)):

        @pl.when(owner & (x == xx))
        def _(copies=copies):
            for cp in copies:
                cp.wait_send()

    for cp in started:
        cp.wait_send()


def on_device(q, k, v, ld, wr, gate, gain, w):
    toks, feats = q.shape
    heads = feats // HS
    kd, width = w.shape
    rb = toks // (NY * NC)
    tile = width // NT_OUT
    anyspec = pl.BlockSpec(memory_space=pl.ANY)
    vmem, dma = pltpu.VMEM, pltpu.SemaphoreType.DMA
    out = jax.ShapeDtypeStruct((rb, width), bf16)
    own, one, two = pl.pallas_call(
        kernel,
        in_specs=[anyspec] * 8,
        out_specs=[anyspec] * 3,
        out_shape=[out] * 3,
        scratch_shapes=[
            vmem((toks, feats), bf16),
            vmem((toks, feats), bf16),
            vmem((toks, feats), bf16),
            vmem((toks, feats), f32),
            vmem((heads, toks), f32),
            vmem((NY, NC, rb, feats), bf16),
            vmem((1, HS), f32),
            vmem((NC, NY * rb, feats), bf16),
            vmem((NC, NY * rb, feats), f32),
            vmem((heads, MSG, HS), bf16),
            vmem((NZ, MSG, HS), bf16),
            vmem((NZ, HS, HS), bf16),
            vmem((NZ, HS, HS), f32),
            vmem((HS, HS), bf16),
            vmem((HS, HS), bf16),
            vmem((2 * HS, HS), bf16),
            vmem((2, 2 * HS, HS), bf16),
            vmem((HS, HS), bf16),
            vmem((NZ, HS, HS), bf16),
            vmem((heads, HS, HS), bf16),
            vmem((NC, NY * rb, kd), bf16),
            vmem((NY * rb, kd), bf16),
            vmem((NC, kd, width), bf16),
            vmem((NT_OUT // 2, NY * rb, 2 * tile), f32),
            vmem((NT_OUT, NY, rb, tile), bf16),
            vmem((NT_OUT, rb, tile), bf16),
            dma((7,)),
            dma((heads,)),
            dma((NZ,)),
            dma((3,)),
            dma((3,)),
            dma((NZ,)),
            dma((heads,)),
            dma((heads,)),
            dma((heads,)),
            dma,
            dma,
            dma,
            dma((3, NT_OUT)),
            dma((NT_OUT,)),
            dma((2, NT_OUT)),
            dma((NT_OUT,)),
        ],
        compiler_params=pltpu.CompilerParams(
            collective_id=0, has_side_effects=True, vmem_limit_bytes=56 << 20
        ),
        name="delta_layer",
    )(q, k, v, ld, wr.T, gate.reshape(NY, NC, rb, feats), gain.reshape(1, HS), w)
    return (own.astype(f32) + one.astype(f32) + two.astype(f32)).astype(bf16)


def solution(mesh):
    in_specs = (
        P("ctx", "head"),
        P("ctx", "head"),
        P("ctx", "head"),
        P("ctx", "head"),
        P("ctx", "head"),
        P("ctx", "head"),
        P(),
        P("head", None),
    )
    out_specs = P(("ctx", "head"), None)
    return jax.shard_map(
        on_device, mesh=mesh, in_specs=in_specs, out_specs=out_specs, check_vma=False
    )
```

```python
import jax
import jax.numpy as jnp
from jax import lax
from jax.experimental import pallas as pl
from jax.experimental.pallas import tpu as pltpu
from jax.sharding import PartitionSpec as P

HS = 128
C = 64
W = 2 * C
NX, NZ = 4, 8
NY, NC = 4, 2
MSG = 2 * HS + 16
OWNER = (0, 4, 2, 6)
NT_OUT = 6
MESH = pl.DeviceIdType.MESH
bf16, f32 = jnp.bfloat16, jnp.float32
NN, NT, TN = ((1,), (0,)), ((1,), (1,)), ((0,), (0,))


def mm(a, b, dims=NN):
    return lax.dot_general(
        a.astype(bf16), b.astype(bf16), (dims, ((), ())), preferred_element_type=f32
    )


def masks():
    i = lax.broadcasted_iota(jnp.int32, (W, W), 0)
    j = lax.broadcasted_iota(jnp.int32, (W, W), 1)
    return i, j


def prep_maps(n_heads, n_blocks, read):
    i, j = masks()
    lower = ((i >= j) & ((i // C) == (j // C))).astype(bf16)
    eye = (i == j).astype(f32)
    zero = jnp.zeros((W, W), bf16)
    blocks = [dict(h=h, p=p) for h in range(n_heads) for p in range(n_blocks)]
    for b in blocks:
        ld = read("ld", b)
        hi = ld.astype(bf16)
        lo = (ld - hi.astype(f32)).astype(bf16)
        b["cum"] = mm(lower, hi) + mm(lower, lo)
    for b in blocks:
        kf = read("k", b).astype(f32)
        unit = kf * lax.rsqrt(jnp.sum(kf * kf, axis=-1, keepdims=True) + 1e-6)
        cum = b.pop("cum")
        b["beta"] = read("beta", b)
        e1, e2 = cum[C - 1 : C], cum[W - 1 : W]
        d1, d2 = jnp.exp(e1), jnp.exp(e2)
        grow = jnp.exp(cum)
        back = (unit * jnp.exp(-cum)).astype(bf16)
        kn = b["beta"] * (unit * grow)
        ke1 = unit[:C] * jnp.exp(e1 - cum[:C])
        ke2 = unit[C:] * jnp.exp(e2 - cum[C:])
        knb = kn.astype(bf16)
        earlier = jnp.concatenate([ke1.astype(bf16), back[C:]], 0)
        a = jnp.concatenate([mm(knb[:C], back, NT), mm(knb[C:], earlier, NT)], 0)
        b["a"] = jnp.where(i > j, a, 0.0).astype(bf16)
        b["left"] = jnp.concatenate([knb[:C], (kn[C:] * d1).astype(bf16)], 0)
        b["ke"] = jnp.concatenate([(ke1 * d2).astype(bf16), ke2.astype(bf16)], 0)
        b["d"] = d1 * d2
        b["later"] = (grow, d1, back, earlier)
    size = 1
    while size < W:
        mask = ((i // size) % 2 == 1) & ((j // size) == (i // size) - 1)
        odd = range(size, W, 2 * size)
        if size >= 16:
            pick = jnp.concatenate([mask[lo : lo + size] for lo in odd], 0)
            for b in blocks:
                step = jnp.concatenate([b["a"][lo : lo + size] for lo in odd], 0)
                st = mm(jnp.where(pick, step, zero[: W // 2]), b["t"]).astype(bf16)
                full = []
                for n in range(len(odd)):
                    full += [zero[:size], st[n * size : (n + 1) * size]]
                b["st"] = jnp.concatenate(full, 0)
            for b in blocks:
                rows = jnp.concatenate([b["t"][lo : lo + size] for lo in odd], 0)
                rows = rows - mm(rows, b["st"])
                full = []
                for n, lo in enumerate(odd):
                    full += [b["t"][lo - size : lo], rows[n * size : (n + 1) * size]]
                b["t"] = jnp.concatenate(full, 0)
            size *= 2
            continue
        for b in blocks:
            step = jnp.where(mask, b["a"], zero)
            b["st"] = step if size == 1 else mm(step, b["t"]).astype(bf16)
        for b in blocks:
            b["t"] = eye - b["st"].astype(f32) if size == 1 else b["t"] - mm(b["t"], b["st"])
        size *= 2
    for b in blocks:
        right = (b["beta"] * read("v", b).astype(f32)).astype(bf16)
        b["y"] = mm(b["t"], jnp.concatenate([b["left"], right], 1)).astype(bf16)
    for b in blocks:
        b["yk"] = mm(b["y"], b["ke"], TN)
    x = [None] * n_heads
    total = [None] * n_heads
    for p in range(n_blocks):
        for h in range(n_heads):
            b = blocks[h * n_blocks + p]
            if p == 0:
                x[h] = jnp.concatenate([eye * b["d"] - b["yk"][:HS], b["yk"][HS:]], 0)
                total[h] = b["d"]
            else:
                b["x"] = x[h].astype(bf16)
                nx = x[h] * b["d"] - mm(b["x"], b["yk"][:HS])
                x[h] = jnp.concatenate([nx[:HS], nx[HS:] + b["yk"][HS:]], 0)
                total[h] = total[h] * b["d"]
    ends = [(eye * total[h] - x[h][:HS], x[h][HS:], total[h]) for h in range(n_heads)]
    return blocks, ends


def prep_reads(blocks, read, write):
    i, j = masks()
    for b in blocks:
        grow, d1, back, earlier = b["later"]
        qn = read("q", b).astype(f32) * grow
        qnb = qn.astype(bf16)
        r = jnp.concatenate([mm(qnb[:C], back, NT), mm(qnb[C:], earlier, NT)], 0)
        b["r"] = jnp.where(i >= j, r, 0.0).astype(bf16)
        b["qn"] = jnp.concatenate([qn[:C], qn[C:] * d1], 0)
    for b in blocks:
        b["ry"] = mm(b["r"], b["y"])
    for b in blocks:
        qe, local = b["qn"] - b["ry"][:, :HS], b["ry"][:, HS:]
        if "x" in b:
            o = mm(qe, b["x"], NT)
            qe, local = o[:, :HS], o[:, HS:] + local
        write(b, qe.astype(bf16), local)


def kernel(
    q_hbm,
    k_hbm,
    v_hbm,
    ld_hbm,
    wr_hbm,
    gate_hbm,
    gain_hbm,
    w_hbm,
    own_hbm,
    prev_hbm,
    next_hbm,
    q_ref,
    k_ref,
    v_ref,
    ld_ref,
    wr_ref,
    gate_ref,
    gain_ref,
    qd_ref,
    loc_ref,
    msg_ref,
    rmsg,
    pre_map,
    pre_state,
    s_out,
    s_in,
    t_out,
    t_in,
    s0,
    sin_out,
    sin,
    gated,
    gsib,
    weights,
    acc,
    psend,
    pvia,
    in_sem,
    m_send,
    m_recv,
    x_send,
    x_recv,
    s_send,
    s_recv,
    g_send,
    g_recv,
    w_sem,
    w_send,
    w_recv,
    p_send,
    v_recv,
    p_recv,
    o_sem,
):
    outs = (prev_hbm, next_hbm)
    ctx = lax.axis_index("ctx")
    head = lax.axis_index("head")
    x, z = ctx // NZ, ctx % NZ
    y, core = head // NC, head % NC
    feats = qd_ref.shape[2]
    heads = feats // HS
    rows = qd_ref.shape[1] // NY
    sib = (ctx, y * NC + (1 - core))

    def zdev(zz):
        return (x * NZ + zz, head)

    ynext = (ctx, lax.rem(y + 1, NY) * NC + core)
    yprev = (ctx, lax.rem(y + NY - 1, NY) * NC + core)

    def xdev(xx):
        return (xx * NZ + z, head)

    barrier = pltpu.get_barrier_semaphore()
    peers = [zdev(lax.rem(z + s, NZ)) for s in range(1, NZ)] + [ynext, yprev, sib]
    peers += [xdev(lax.rem(x + s, NX)) for s in range(1, NX)]
    loads = []
    for n, (src, dst) in enumerate(
        (
            (ld_hbm, ld_ref),
            (k_hbm, k_ref),
            (wr_hbm, wr_ref),
            (v_hbm, v_ref),
            (q_hbm, q_ref),
            (gate_hbm, gate_ref),
            (gain_hbm, gain_ref),
        )
    ):
        cp = pltpu.make_async_copy(src, dst, in_sem.at[n])
        loads.append(cp)
        if n < 5:
            cp.start()
    wown = pltpu.make_async_copy(w_hbm, weights.at[core], w_sem)
    for peer in peers:
        pl.semaphore_signal(barrier, inc=1, device_id=peer, device_id_type=MESH)

    def remote(src, dst, send, recv, dev):
        return pltpu.make_async_remote_copy(
            src_ref=src, dst_ref=dst, send_sem=send, recv_sem=recv, device_id=dev, device_id_type=MESH
        )

    waited = set()

    def read(name, b):
        for n in dict(ld=(0,), k=(1,), beta=(2,), v=(3,), q=(4,))[name]:
            if n not in waited:
                waited.add(n)
                loads[n].wait()
        at = (slice(b["p"] * W, (b["p"] + 1) * W), slice(b["h"] * HS, (b["h"] + 1) * HS))
        if name == "beta":
            if "beta" not in cache:
                cache["beta"] = wr_ref[...].T
            return cache["beta"][at[0], b["h"] : b["h"] + 1]
        return dict(ld=ld_ref, k=k_ref, v=v_ref, q=q_ref)[name][at]

    cache = {}
    ti = lax.broadcasted_iota(jnp.int32, (MSG - 2 * HS, HS), 0)
    blocks, ends = prep_maps(heads, q_ref.shape[0] // W, read)
    for h, (take, state, total) in enumerate(ends):
        t1 = total.astype(bf16).astype(f32)
        t2 = (total - t1).astype(bf16).astype(f32)
        t3 = total - t1 - t2
        tail = jnp.where(ti == 0, t1, jnp.where(ti == 1, t2, jnp.where(ti == 2, t3, 0.0)))
        msg_ref[h, :HS] = take.astype(bf16)
        msg_ref[h, HS : 2 * HS] = state.astype(bf16)
        msg_ref[h, 2 * HS :] = tail.astype(bf16)

    pl.semaphore_wait(barrier, len(peers))

    sends = []
    for h in range(heads):
        sends.append(remote(msg_ref.at[h], rmsg.at[z], m_send.at[h], m_recv.at[z], zdev(OWNER[h] + core)))

        @pl.when(z != OWNER[h] + core)
        def _(h=h):
            sends[h].start()

        @pl.when(z == OWNER[h] + core)
        def _(h=h):
            rmsg[z] = msg_ref[h]

    wsib = remote(w_hbm, weights.at[core], w_send, w_recv, sib)
    wsib.start()
    for cp in loads[5:]:
        cp.start()
    wown.start()

    owner = z % 2 == core
    slot = (z // 4) + 2 * ((z // 2) % 2)

    def write(b, qd, local):
        cols = slice(b["h"] * HS, (b["h"] + 1) * HS)
        lo = b["p"] * W
        while lo < (b["p"] + 1) * W:
            jj = lo // rows
            hi = min((b["p"] + 1) * W, (jj + 1) * rows)
            to = (jj // NC) * rows + lo - jj * rows
            qd_ref[jj % NC, to : to + hi - lo, cols] = qd[lo - b["p"] * W : hi - b["p"] * W]
            loc_ref[jj % NC, to : to + hi - lo, cols] = local[lo - b["p"] * W : hi - b["p"] * W]
            lo = hi

    prep_reads(blocks, read, write)
    for n in (5, 6):
        loads[n].wait()
    states = [remote(s_out, s_in, x_send.at[xx - 1], x_recv.at[0], xdev(xx)) for xx in (3, 2, 1)]
    totals1 = [remote(t_out, t_in.at[0], x_send.at[xx - 1], x_recv.at[1], xdev(xx)) for xx in (3, 2)]
    totals2 = [remote(t_out, t_in.at[1], x_send.at[xx - 1], x_recv.at[2], xdev(xx)) for xx in (3,)]
    backs = []
    for s in (4, 3, 5, 2, 6, 1, 7):
        zz = lax.rem(z + s, NZ)
        backs.append((zz, remote(sin_out.at[zz], sin.at[slot], s_send.at[s], s_recv.at[slot], zdev(zz))))

    @pl.when(owner)
    def _():
        ei = lax.broadcasted_iota(jnp.int32, (2 * HS, HS), 0)
        ej = lax.broadcasted_iota(jnp.int32, (2 * HS, HS), 1)
        run = (ei == ej).astype(f32)
        for zz in range(NZ):

            @pl.when(z != zz)
            def _(zz=zz):
                remote(msg_ref.at[0], rmsg.at[zz], m_send.at[0], m_recv.at[zz], zdev(zz)).wait_recv()

            pre_map[zz] = run[:HS].astype(bf16)
            pre_state[zz] = run[HS:]
            d = jnp.sum(rmsg[zz, 2 * HS :, :].astype(f32), axis=0, keepdims=True)
            new = run * d - mm(run, rmsg[zz, :HS, :])
            run = jnp.concatenate([new[:HS], new[HS:] + rmsg[zz, HS : 2 * HS, :].astype(f32)], 0)

        @pl.when(x == 0)
        def _():
            s_out[...] = run[HS:].astype(bf16)
            for cp in states:
                cp.start()
            s0[...] = jnp.zeros_like(s0)

        @pl.when((x == 1) | (x == 2))
        def _():
            t_out[...] = run.astype(bf16)

        @pl.when(x == 1)
        def _():
            for cp in totals1:
                cp.start()
            states[0].wait_recv()
            s0[...] = s_in[...]

        @pl.when(x == 2)
        def _():
            totals2[0].start()

        @pl.when(x >= 2)
        def _():
            states[0].wait_recv()
            totals1[0].wait_recv()
            s0[...] = (mm(s_in[...], t_in[0, :HS]) + t_in[0, HS:].astype(f32)).astype(bf16)

        @pl.when(x == 3)
        def _():
            totals2[0].wait_recv()
            s0[...] = (mm(s0[...], t_in[1, :HS]) + t_in[1, HS:].astype(f32)).astype(bf16)

        s0v = s0[...]
        for zz in range(NZ):
            sin_out[zz] = (mm(s0v, pre_map[zz]) + pre_state[zz]).astype(bf16)
        for zz, cp in backs:
            cp.start()
        sin[slot] = sin_out[z]

    def read(part, h):
        cols = slice(h * HS, (h + 1) * HS)
        att = mm(qd_ref[part, :, cols], sin[h], NT) + loc_ref[part, :, cols]
        ms = jnp.mean(att * att, axis=-1, keepdims=True)
        gate = jax.nn.sigmoid(gate_ref[:, part, :, cols].astype(f32).reshape(NY * rows, HS))
        return (att * lax.rsqrt(ms + 1e-5) * gain_ref[...] * gate).astype(bf16)

    gcopies = []
    for pair in range(heads // 2):
        two = (2 * pair, 2 * pair + 1)
        for h in two:

            @pl.when(z != OWNER[h] + core)
            def _(h=h):
                remote(sin_out.at[0], sin.at[h], s_send.at[0], s_recv.at[h], zdev(OWNER[h] + core)).wait_recv()

        out = [read(1 - core, h) for h in two]
        cols = slice(two[0] * HS, (two[1] + 1) * HS)
        gated[1 - core, :, cols] = jnp.concatenate(out, 1)
        cp = remote(gated.at[1 - core, :, cols], gsib.at[:, cols], g_send.at[pair], g_recv.at[pair], sib)
        cp.start()
        gcopies.append(cp)
    for h in range(heads):
        gated[core, :, h * HS : (h + 1) * HS] = read(core, h)

    started = []
    tile = weights.shape[2] // NT_OUT
    wide = 2 * tile
    wown.wait()
    mine = gated[core]
    for t in range(NT_OUT // 2):
        acc[t] = mm(mine, weights[core, :, t * wide : (t + 1) * wide])
    wsib.wait()
    for cp in gcopies:
        cp.wait()
    other = gsib[...]
    y1, y2, y3 = [lax.rem(y + s, NY) for s in range(1, NY)]
    for t in range(NT_OUT // 2):
        val = acc[t] + mm(other, weights[1 - core, :, t * wide : (t + 1) * wide])
        val = val.reshape(NY, rows, wide).astype(bf16)
        for u in range(2):
            psend[2 * t + u] = val[:, :, u * tile : (u + 1) * tile]
        for u in range(2):
            n = 2 * t + u
            cp = remote(psend.at[n, y2], pvia.at[n], p_send.at[0, n], v_recv.at[n], (ynext, yprev)[u])
            cp.start()
            started.append(cp)
    for t in range(NT_OUT):
        u = t % 2
        cp = remote(
            psend.at[t, (y3, y1)[u]],
            outs[1 - u].at[:, t * tile : (t + 1) * tile],
            p_send.at[1, t],
            p_recv.at[1 - u, t],
            (yprev, ynext)[u],
        )
        cp.start()
        started.append(cp)
    locals_ = []
    for t in range(NT_OUT):
        cp = pltpu.make_async_copy(psend.at[t, y], own_hbm.at[:, t * tile : (t + 1) * tile], o_sem.at[t])
        cp.start()
        locals_.append(cp)
    for t in range(NT_OUT // 2):
        for u in range(2):
            n = 2 * t + u
            remote(
                psend.at[n, 0], pvia.at[n], p_send.at[0, n], v_recv.at[n], (yprev, ynext)[u]
            ).wait_recv()
        for u in range(2):
            n = 2 * t + u
            near = (y1, y3)[u]
            psend[n, near] = (psend[n, near].astype(f32) + pvia[n].astype(f32)).astype(bf16)
        for u in range(2):
            n = 2 * t + u
            cp = remote(
                psend.at[n, (y1, y3)[u]],
                outs[u].at[:, n * tile : (n + 1) * tile],
                p_send.at[2, n],
                p_recv.at[u, n],
                (ynext, yprev)[u],
            )
            cp.start()
            started.append(cp)
    for t in range(NT_OUT):
        for side in range(2):
            cols = slice(t * tile, (t + 1) * tile)
            remote(
                psend.at[t, 0], outs[side].at[:, cols], p_send.at[0, t], p_recv.at[side, t], (yprev, ynext)[side]
            ).wait_recv()
    for cp in locals_:
        cp.wait()

    for h in range(heads):

        @pl.when(z != OWNER[h] + core)
        def _(h=h):
            sends[h].wait_send()

    @pl.when(owner)
    def _():
        for _, cp in backs:
            cp.wait_send()

    for xx, copies in enumerate((states, totals1, totals2)):

        @pl.when(owner & (x == xx))
        def _(copies=copies):
            for cp in copies:
                cp.wait_send()

    for cp in started:
        cp.wait_send()


def on_device(q, k, v, ld, wr, gate, gain, w):
    toks, feats = q.shape
    heads = feats // HS
    kd, width = w.shape
    rb = toks // (NY * NC)
    tile = width // NT_OUT
    anyspec = pl.BlockSpec(memory_space=pltpu.HBM)
    vmem, dma = pltpu.VMEM, pltpu.SemaphoreType.DMA
    out = jax.ShapeDtypeStruct((rb, width), bf16)
    own, one, two = pl.pallas_call(
        kernel,
        in_specs=[anyspec] * 8,
        out_specs=[pl.BlockSpec(memory_space=pltpu.VMEM)] * 3,
        out_shape=[out] * 3,
        scratch_shapes=[
            vmem((toks, feats), bf16),
            vmem((toks, feats), bf16),
            vmem((toks, feats), bf16),
            vmem((toks, feats), f32),
            vmem((heads, toks), f32),
            vmem((NY, NC, rb, feats), bf16),
            vmem((1, HS), f32),
            vmem((NC, NY * rb, feats), bf16),
            vmem((NC, NY * rb, feats), f32),
            vmem((heads, MSG, HS), bf16),
            vmem((NZ, MSG, HS), bf16),
            vmem((NZ, HS, HS), bf16),
            vmem((NZ, HS, HS), f32),
            vmem((HS, HS), bf16),
            vmem((HS, HS), bf16),
            vmem((2 * HS, HS), bf16),
            vmem((2, 2 * HS, HS), bf16),
            vmem((HS, HS), bf16),
            vmem((NZ, HS, HS), bf16),
            vmem((heads, HS, HS), bf16),
            vmem((NC, NY * rb, kd), bf16),
            vmem((NY * rb, kd), bf16),
            vmem((NC, kd, width), bf16),
            vmem((NT_OUT // 2, NY * rb, 2 * tile), f32),
            vmem((NT_OUT, NY, rb, tile), bf16),
            vmem((NT_OUT, rb, tile), bf16),
            dma((7,)),
            dma((heads,)),
            dma((NZ,)),
            dma((3,)),
            dma((3,)),
            dma((NZ,)),
            dma((heads,)),
            dma((heads,)),
            dma((heads,)),
            dma,
            dma,
            dma,
            dma((3, NT_OUT)),
            dma((NT_OUT,)),
            dma((2, NT_OUT)),
            dma((NT_OUT,)),
        ],
        compiler_params=pltpu.CompilerParams(
            collective_id=0, has_side_effects=True, vmem_limit_bytes=40 << 20
        ),
        name="delta_layer",
    )(*[pltpu.with_memory_space_constraint(a, pltpu.HBM) for a in (q, k, v, ld, wr.T, gate.reshape(NY, NC, rb, feats), gain.reshape(1, HS), w)])
    return (own.astype(f32) + one.astype(f32) + two.astype(f32)).astype(bf16)


def solution(mesh):
    in_specs = (
        P("ctx", "head"),
        P("ctx", "head"),
        P("ctx", "head"),
        P("ctx", "head"),
        P("ctx", "head"),
        P("ctx", "head"),
        P(),
        P("head", None),
    )
    out_specs = P(("ctx", "head"), None)
    return jax.shard_map(
        on_device, mesh=mesh, in_specs=in_specs, out_specs=out_specs, check_vma=False
    )
```

```python
import jax
import jax.numpy as jnp
from jax import lax
from jax.experimental import pallas as pl
from jax.experimental.pallas import tpu as pltpu
from jax.sharding import PartitionSpec as P

HS = 128
C = 64
W = 2 * C
NX, NZ = 4, 8
NY, NC = 4, 2
MSG = 2 * HS + 16
OWNER = (0, 4, 2, 6)
NT_OUT = 6
MESH = pl.DeviceIdType.MESH
bf16, f32 = jnp.bfloat16, jnp.float32
NN, NT, TN = ((1,), (0,)), ((1,), (1,)), ((0,), (0,))


def mm(a, b, dims=NN):
    return lax.dot_general(
        a.astype(bf16), b.astype(bf16), (dims, ((), ())), preferred_element_type=f32
    )


def masks():
    i = lax.broadcasted_iota(jnp.int32, (W, W), 0)
    j = lax.broadcasted_iota(jnp.int32, (W, W), 1)
    return i, j


def prep_maps(n_heads, n_blocks, read):
    i, j = masks()
    lower = ((i >= j) & ((i // C) == (j // C))).astype(bf16)
    eye = (i == j).astype(f32)
    zero = jnp.zeros((W, W), bf16)
    blocks = [dict(h=h, p=p) for h in range(n_heads) for p in range(n_blocks)]
    for b in blocks:
        ld = read("ld", b)
        hi = ld.astype(bf16)
        lo = (ld - hi.astype(f32)).astype(bf16)
        b["cum"] = mm(lower, hi) + mm(lower, lo)
    for b in blocks:
        kf = read("k", b).astype(f32)
        unit = kf * lax.rsqrt(jnp.sum(kf * kf, axis=-1, keepdims=True) + 1e-6)
        cum = b.pop("cum")
        b["beta"] = read("beta", b)
        e1, e2 = cum[C - 1 : C], cum[W - 1 : W]
        d1, d2 = jnp.exp(e1), jnp.exp(e2)
        grow = jnp.exp(cum)
        back = (unit * jnp.exp(-cum)).astype(bf16)
        kn = b["beta"] * (unit * grow)
        ke1 = unit[:C] * jnp.exp(e1 - cum[:C])
        ke2 = unit[C:] * jnp.exp(e2 - cum[C:])
        knb = kn.astype(bf16)
        earlier = jnp.concatenate([ke1.astype(bf16), back[C:]], 0)
        a = jnp.concatenate([mm(knb[:C], back, NT), mm(knb[C:], earlier, NT)], 0)
        b["a"] = jnp.where(i > j, a, 0.0).astype(bf16)
        b["left"] = jnp.concatenate([knb[:C], (kn[C:] * d1).astype(bf16)], 0)
        b["ke"] = jnp.concatenate([(ke1 * d2).astype(bf16), ke2.astype(bf16)], 0)
        b["d"] = d1 * d2
        b["later"] = (grow, d1, back, earlier)
    size = 1
    while size < W:
        mask = ((i // size) % 2 == 1) & ((j // size) == (i // size) - 1)
        odd = range(size, W, 2 * size)
        if size >= 16:
            pick = jnp.concatenate([mask[lo : lo + size] for lo in odd], 0)
            for b in blocks:
                step = jnp.concatenate([b["a"][lo : lo + size] for lo in odd], 0)
                st = mm(jnp.where(pick, step, zero[: W // 2]), b["t"]).astype(bf16)
                full = []
                for n in range(len(odd)):
                    full += [zero[:size], st[n * size : (n + 1) * size]]
                b["st"] = jnp.concatenate(full, 0)
            for b in blocks:
                rows = jnp.concatenate([b["t"][lo : lo + size] for lo in odd], 0)
                rows = rows - mm(rows, b["st"])
                full = []
                for n, lo in enumerate(odd):
                    full += [b["t"][lo - size : lo], rows[n * size : (n + 1) * size]]
                b["t"] = jnp.concatenate(full, 0)
            size *= 2
            continue
        for b in blocks:
            step = jnp.where(mask, b["a"], zero)
            b["st"] = step if size == 1 else mm(step, b["t"]).astype(bf16)
        for b in blocks:
            b["t"] = eye - b["st"].astype(f32) if size == 1 else b["t"] - mm(b["t"], b["st"])
        size *= 2
    for b in blocks:
        right = (b["beta"] * read("v", b).astype(f32)).astype(bf16)
        b["y"] = mm(b["t"], jnp.concatenate([b["left"], right], 1)).astype(bf16)
    for b in blocks:
        b["yk"] = mm(b["y"], b["ke"], TN)
    x = [None] * n_heads
    total = [None] * n_heads
    for p in range(n_blocks):
        for h in range(n_heads):
            b = blocks[h * n_blocks + p]
            if p == 0:
                x[h] = jnp.concatenate([eye * b["d"] - b["yk"][:HS], b["yk"][HS:]], 0)
                total[h] = b["d"]
            else:
                b["x"] = x[h].astype(bf16)
                nx = x[h] * b["d"] - mm(b["x"], b["yk"][:HS])
                x[h] = jnp.concatenate([nx[:HS], nx[HS:] + b["yk"][HS:]], 0)
                total[h] = total[h] * b["d"]
    ends = [(eye * total[h] - x[h][:HS], x[h][HS:], total[h]) for h in range(n_heads)]
    return blocks, ends


def prep_reads(blocks, read, write):
    i, j = masks()
    for b in blocks:
        grow, d1, back, earlier = b["later"]
        qn = read("q", b).astype(f32) * grow
        qnb = qn.astype(bf16)
        r = jnp.concatenate([mm(qnb[:C], back, NT), mm(qnb[C:], earlier, NT)], 0)
        b["r"] = jnp.where(i >= j, r, 0.0).astype(bf16)
        b["qn"] = jnp.concatenate([qn[:C], qn[C:] * d1], 0)
    for b in blocks:
        b["ry"] = mm(b["r"], b["y"])
    for b in blocks:
        qe, local = b["qn"] - b["ry"][:, :HS], b["ry"][:, HS:]
        if "x" in b:
            o = mm(qe, b["x"], NT)
            qe, local = o[:, :HS], o[:, HS:] + local
        write(b, qe.astype(bf16), local)


def kernel(
    q_hbm,
    k_hbm,
    v_hbm,
    ld_hbm,
    wr_hbm,
    gate_hbm,
    gain_hbm,
    w_hbm,
    own_hbm,
    prev_hbm,
    next_hbm,
    q_ref,
    k_ref,
    v_ref,
    ld_ref,
    wr_ref,
    gate_ref,
    gain_ref,
    qd_ref,
    loc_ref,
    msg_ref,
    rmsg,
    pre_map,
    pre_state,
    s_out,
    s_in,
    t_out,
    t_in,
    s0,
    sin_out,
    sin,
    gated,
    gsib,
    weights,
    acc,
    psend,
    pvia,
    in_sem,
    m_send,
    m_recv,
    x_send,
    x_recv,
    s_send,
    s_recv,
    g_send,
    g_recv,
    w_sem,
    w_send,
    w_recv,
    p_send,
    v_recv,
    p_recv,
    o_sem,
):
    outs = (prev_hbm, next_hbm)
    ctx = lax.axis_index("ctx")
    head = lax.axis_index("head")
    x, z = ctx // NZ, ctx % NZ
    y, core = head // NC, head % NC
    feats = qd_ref.shape[2]
    heads = feats // HS
    rows = qd_ref.shape[1] // NY
    sib = (ctx, y * NC + (1 - core))

    def zdev(zz):
        return (x * NZ + zz, head)

    ynext = (ctx, lax.rem(y + 1, NY) * NC + core)
    yprev = (ctx, lax.rem(y + NY - 1, NY) * NC + core)

    def xdev(xx):
        return (xx * NZ + z, head)

    barrier = pltpu.get_barrier_semaphore()
    peers = [zdev(lax.rem(z + s, NZ)) for s in range(1, NZ)] + [ynext, yprev, sib]
    peers += [xdev(lax.rem(x + s, NX)) for s in range(1, NX)]
    loads = []
    for n, (src, dst) in enumerate(
        (
            (ld_hbm, ld_ref),
            (k_hbm, k_ref),
            (wr_hbm, wr_ref),
            (v_hbm, v_ref),
            (q_hbm, q_ref),
            (gate_hbm, gate_ref),
            (gain_hbm, gain_ref),
        )
    ):
        cp = pltpu.make_async_copy(src, dst, in_sem.at[n])
        loads.append(cp)
        if n < 5:
            cp.start()
    wown = pltpu.make_async_copy(w_hbm, weights.at[core], w_sem)
    for peer in peers:
        pl.semaphore_signal(barrier, inc=1, device_id=peer, device_id_type=MESH)

    def remote(src, dst, send, recv, dev):
        return pltpu.make_async_remote_copy(
            src_ref=src, dst_ref=dst, send_sem=send, recv_sem=recv, device_id=dev, device_id_type=MESH
        )

    waited = set()

    def read(name, b):
        for n in dict(ld=(0,), k=(1,), beta=(2,), v=(3,), q=(4,))[name]:
            if n not in waited:
                waited.add(n)
                loads[n].wait()
        at = (slice(b["p"] * W, (b["p"] + 1) * W), slice(b["h"] * HS, (b["h"] + 1) * HS))
        if name == "beta":
            if "beta" not in cache:
                cache["beta"] = wr_ref[...].T
            return cache["beta"][at[0], b["h"] : b["h"] + 1]
        return dict(ld=ld_ref, k=k_ref, v=v_ref, q=q_ref)[name][at]

    cache = {}
    ti = lax.broadcasted_iota(jnp.int32, (MSG - 2 * HS, HS), 0)
    blocks, ends = prep_maps(heads, q_ref.shape[0] // W, read)
    pl.semaphore_wait(barrier, len(peers))
    sends = []
    for h, (take, state, total) in enumerate(ends):
        t1 = total.astype(bf16).astype(f32)
        t2 = (total - t1).astype(bf16).astype(f32)
        t3 = total - t1 - t2
        tail = jnp.where(ti == 0, t1, jnp.where(ti == 1, t2, jnp.where(ti == 2, t3, 0.0)))
        msg_ref[h, :HS] = take.astype(bf16)
        msg_ref[h, HS : 2 * HS] = state.astype(bf16)
        msg_ref[h, 2 * HS :] = tail.astype(bf16)
        sends.append(remote(msg_ref.at[h], rmsg.at[z], m_send.at[h], m_recv.at[z], zdev(OWNER[h] + core)))

        @pl.when(z != OWNER[h] + core)
        def _(h=h):
            sends[h].start()

        @pl.when(z == OWNER[h] + core)
        def _(h=h):
            rmsg[z] = msg_ref[h]

    wsib = remote(w_hbm, weights.at[core], w_send, w_recv, sib)
    for cp in loads[5:]:
        cp.start()

    owner = z % 2 == core
    slot = (z // 4) + 2 * ((z // 2) % 2)

    def write(b, qd, local):
        cols = slice(b["h"] * HS, (b["h"] + 1) * HS)
        lo = b["p"] * W
        while lo < (b["p"] + 1) * W:
            jj = lo // rows
            hi = min((b["p"] + 1) * W, (jj + 1) * rows)
            to = (jj // NC) * rows + lo - jj * rows
            qd_ref[jj % NC, to : to + hi - lo, cols] = qd[lo - b["p"] * W : hi - b["p"] * W]
            loc_ref[jj % NC, to : to + hi - lo, cols] = local[lo - b["p"] * W : hi - b["p"] * W]
            lo = hi

    prep_reads(blocks, read, write)
    wsib.start()
    wown.start()
    for n in (5, 6):
        loads[n].wait()
    states = [remote(s_out, s_in, x_send.at[xx - 1], x_recv.at[0], xdev(xx)) for xx in (3, 2, 1)]
    totals1 = [remote(t_out, t_in.at[0], x_send.at[xx - 1], x_recv.at[1], xdev(xx)) for xx in (3, 2)]
    totals2 = [remote(t_out, t_in.at[1], x_send.at[xx - 1], x_recv.at[2], xdev(xx)) for xx in (3,)]
    backs = []
    for s in (4, 3, 5, 2, 6, 1, 7):
        zz = lax.rem(z + s, NZ)
        backs.append((zz, remote(sin_out.at[zz], sin.at[slot], s_send.at[s], s_recv.at[slot], zdev(zz))))

    @pl.when(owner)
    def _():
        ei = lax.broadcasted_iota(jnp.int32, (2 * HS, HS), 0)
        ej = lax.broadcasted_iota(jnp.int32, (2 * HS, HS), 1)
        run = (ei == ej).astype(f32)
        for zz in range(NZ):

            @pl.when(z != zz)
            def _(zz=zz):
                remote(msg_ref.at[0], rmsg.at[zz], m_send.at[0], m_recv.at[zz], zdev(zz)).wait_recv()

            pre_map[zz] = run[:HS].astype(bf16)
            pre_state[zz] = run[HS:]
            d = jnp.sum(rmsg[zz, 2 * HS :, :].astype(f32), axis=0, keepdims=True)
            new = run * d - mm(run, rmsg[zz, :HS, :])
            run = jnp.concatenate([new[:HS], new[HS:] + rmsg[zz, HS : 2 * HS, :].astype(f32)], 0)

        @pl.when(x == 0)
        def _():
            s_out[...] = run[HS:].astype(bf16)
            for cp in states:
                cp.start()
            s0[...] = jnp.zeros_like(s0)

        @pl.when((x == 1) | (x == 2))
        def _():
            t_out[...] = run.astype(bf16)

        @pl.when(x == 1)
        def _():
            for cp in totals1:
                cp.start()
            states[0].wait_recv()
            s0[...] = s_in[...]

        @pl.when(x == 2)
        def _():
            totals2[0].start()

        @pl.when(x >= 2)
        def _():
            states[0].wait_recv()
            totals1[0].wait_recv()
            s0[...] = (mm(s_in[...], t_in[0, :HS]) + t_in[0, HS:].astype(f32)).astype(bf16)

        @pl.when(x == 3)
        def _():
            totals2[0].wait_recv()
            s0[...] = (mm(s0[...], t_in[1, :HS]) + t_in[1, HS:].astype(f32)).astype(bf16)

        s0v = s0[...]
        for zz in range(NZ):
            sin_out[zz] = (mm(s0v, pre_map[zz]) + pre_state[zz]).astype(bf16)
        for zz, cp in backs:
            cp.start()
        sin[slot] = sin_out[z]

    def read(part, h):
        cols = slice(h * HS, (h + 1) * HS)
        att = mm(qd_ref[part, :, cols], sin[h], NT) + loc_ref[part, :, cols]
        ms = jnp.mean(att * att, axis=-1, keepdims=True)
        gate = jax.nn.sigmoid(gate_ref[:, part, :, cols].astype(f32).reshape(NY * rows, HS))
        return (att * lax.rsqrt(ms + 1e-5) * gain_ref[...] * gate).astype(bf16)

    gcopies = []
    for pair in range(heads // 2):
        two = (2 * pair, 2 * pair + 1)
        for h in two:

            @pl.when(z != OWNER[h] + core)
            def _(h=h):
                remote(sin_out.at[0], sin.at[h], s_send.at[0], s_recv.at[h], zdev(OWNER[h] + core)).wait_recv()

        out = [read(1 - core, h) for h in two]
        cols = slice(two[0] * HS, (two[1] + 1) * HS)
        gated[1 - core, :, cols] = jnp.concatenate(out, 1)
        cp = remote(gated.at[1 - core, :, cols], gsib.at[:, cols], g_send.at[pair], g_recv.at[pair], sib)
        cp.start()
        gcopies.append(cp)
    for h in range(heads):
        gated[core, :, h * HS : (h + 1) * HS] = read(core, h)

    started = []
    tile = weights.shape[2] // NT_OUT
    wide = 2 * tile
    wown.wait()
    mine = gated[core]
    for t in range(NT_OUT // 2):
        acc[t] = mm(mine, weights[core, :, t * wide : (t + 1) * wide])
    wsib.wait()
    for cp in gcopies:
        cp.wait()
    other = gsib[...]
    y1, y2, y3 = [lax.rem(y + s, NY) for s in range(1, NY)]
    for t in range(NT_OUT // 2):
        val = acc[t] + mm(other, weights[1 - core, :, t * wide : (t + 1) * wide])
        val = val.reshape(NY, rows, wide).astype(bf16)
        for u in range(2):
            psend[2 * t + u] = val[:, :, u * tile : (u + 1) * tile]
        for u in range(2):
            n = 2 * t + u
            cp = remote(psend.at[n, y2], pvia.at[n], p_send.at[0, n], v_recv.at[n], (ynext, yprev)[u])
            cp.start()
            started.append(cp)
    for t in range(NT_OUT):
        u = t % 2
        cp = remote(
            psend.at[t, (y3, y1)[u]],
            outs[1 - u].at[:, t * tile : (t + 1) * tile],
            p_send.at[1, t],
            p_recv.at[1 - u, t],
            (yprev, ynext)[u],
        )
        cp.start()
        started.append(cp)
    locals_ = []
    for t in range(NT_OUT):
        cp = pltpu.make_async_copy(psend.at[t, y], own_hbm.at[:, t * tile : (t + 1) * tile], o_sem.at[t])
        cp.start()
        locals_.append(cp)
    for t in range(NT_OUT // 2):
        for u in range(2):
            n = 2 * t + u
            remote(
                psend.at[n, 0], pvia.at[n], p_send.at[0, n], v_recv.at[n], (yprev, ynext)[u]
            ).wait_recv()
        for u in range(2):
            n = 2 * t + u
            near = (y1, y3)[u]
            psend[n, near] = (psend[n, near].astype(f32) + pvia[n].astype(f32)).astype(bf16)
        for u in range(2):
            n = 2 * t + u
            cp = remote(
                psend.at[n, (y1, y3)[u]],
                outs[u].at[:, n * tile : (n + 1) * tile],
                p_send.at[2, n],
                p_recv.at[u, n],
                (ynext, yprev)[u],
            )
            cp.start()
            started.append(cp)
    for t in range(NT_OUT):
        for side in range(2):
            cols = slice(t * tile, (t + 1) * tile)
            remote(
                psend.at[t, 0], outs[side].at[:, cols], p_send.at[0, t], p_recv.at[side, t], (yprev, ynext)[side]
            ).wait_recv()
    for cp in locals_:
        cp.wait()

    for h in range(heads):

        @pl.when(z != OWNER[h] + core)
        def _(h=h):
            sends[h].wait_send()

    @pl.when(owner)
    def _():
        for _, cp in backs:
            cp.wait_send()

    for xx, copies in enumerate((states, totals1, totals2)):

        @pl.when(owner & (x == xx))
        def _(copies=copies):
            for cp in copies:
                cp.wait_send()

    for cp in started:
        cp.wait_send()


def on_device(q, k, v, ld, wr, gate, gain, w):
    toks, feats = q.shape
    heads = feats // HS
    kd, width = w.shape
    rb = toks // (NY * NC)
    tile = width // NT_OUT
    anyspec = pl.BlockSpec(memory_space=pltpu.HBM)
    vmem, dma = pltpu.VMEM, pltpu.SemaphoreType.DMA
    out = jax.ShapeDtypeStruct((rb, width), bf16)
    own, one, two = pl.pallas_call(
        kernel,
        in_specs=[anyspec] * 8,
        out_specs=[pl.BlockSpec(memory_space=pltpu.VMEM)] * 3,
        out_shape=[out] * 3,
        scratch_shapes=[
            vmem((toks, feats), bf16),
            vmem((toks, feats), bf16),
            vmem((toks, feats), bf16),
            vmem((toks, feats), f32),
            vmem((heads, toks), f32),
            vmem((NY, NC, rb, feats), bf16),
            vmem((1, HS), f32),
            vmem((NC, NY * rb, feats), bf16),
            vmem((NC, NY * rb, feats), f32),
            vmem((heads, MSG, HS), bf16),
            vmem((NZ, MSG, HS), bf16),
            vmem((NZ, HS, HS), bf16),
            vmem((NZ, HS, HS), f32),
            vmem((HS, HS), bf16),
            vmem((HS, HS), bf16),
            vmem((2 * HS, HS), bf16),
            vmem((2, 2 * HS, HS), bf16),
            vmem((HS, HS), bf16),
            vmem((NZ, HS, HS), bf16),
            vmem((heads, HS, HS), bf16),
            vmem((NC, NY * rb, kd), bf16),
            vmem((NY * rb, kd), bf16),
            vmem((NC, kd, width), bf16),
            vmem((NT_OUT // 2, NY * rb, 2 * tile), f32),
            vmem((NT_OUT, NY, rb, tile), bf16),
            vmem((NT_OUT, rb, tile), bf16),
            dma((7,)),
            dma((heads,)),
            dma((NZ,)),
            dma((3,)),
            dma((3,)),
            dma((NZ,)),
            dma((heads,)),
            dma((heads,)),
            dma((heads,)),
            dma,
            dma,
            dma,
            dma((3, NT_OUT)),
            dma((NT_OUT,)),
            dma((2, NT_OUT)),
            dma((NT_OUT,)),
        ],
        compiler_params=pltpu.CompilerParams(
            collective_id=0, has_side_effects=True, vmem_limit_bytes=40 << 20
        ),
        name="delta_layer",
    )(*[pltpu.with_memory_space_constraint(a, pltpu.HBM) for a in (q, k, v, ld, wr.T, gate.reshape(NY, NC, rb, feats), gain.reshape(1, HS), w)])
    return (own.astype(f32) + one.astype(f32) + two.astype(f32)).astype(bf16)


def solution(mesh):
    in_specs = (
        P("ctx", "head"),
        P("ctx", "head"),
        P("ctx", "head"),
        P("ctx", "head"),
        P("ctx", "head"),
        P("ctx", "head"),
        P(),
        P("head", None),
    )
    out_specs = P(("ctx", "head"), None)
    return jax.shard_map(
        on_device, mesh=mesh, in_specs=in_specs, out_specs=out_specs, check_vma=False
    )
```

```python
import jax
import jax.numpy as jnp
from jax import lax
from jax.experimental import pallas as pl
from jax.experimental.pallas import tpu as pltpu
from jax.sharding import PartitionSpec as P

HS = 128
C = 64
W = 2 * C
NX, NZ = 4, 8
NY, NC = 4, 2
MSG = 2 * HS + 16
OWNER = (0, 4, 2, 6)
NT_OUT = 6
MESH = pl.DeviceIdType.MESH
bf16, f32 = jnp.bfloat16, jnp.float32
NN, NT, TN = ((1,), (0,)), ((1,), (1,)), ((0,), (0,))


def mm(a, b, dims=NN):
    return lax.dot_general(
        a.astype(bf16), b.astype(bf16), (dims, ((), ())), preferred_element_type=f32
    )


def masks():
    i = lax.broadcasted_iota(jnp.int32, (W, W), 0)
    j = lax.broadcasted_iota(jnp.int32, (W, W), 1)
    return i, j


def prep_maps(n_heads, n_blocks, read):
    i, j = masks()
    lower = ((i >= j) & ((i // C) == (j // C))).astype(bf16)
    eye = (i == j).astype(f32)
    zero = jnp.zeros((W, W), bf16)
    blocks = [dict(h=h, p=p) for h in range(n_heads) for p in range(n_blocks)]
    for b in blocks:
        ld = read("ld", b)
        hi = ld.astype(bf16)
        lo = (ld - hi.astype(f32)).astype(bf16)
        b["cum"] = mm(lower, hi) + mm(lower, lo)
    for b in blocks:
        kf = read("k", b).astype(f32)
        unit = kf * lax.rsqrt(jnp.sum(kf * kf, axis=-1, keepdims=True) + 1e-6)
        cum = b.pop("cum")
        b["beta"] = read("beta", b)
        e1, e2 = cum[C - 1 : C], cum[W - 1 : W]
        d1, d2 = jnp.exp(e1), jnp.exp(e2)
        grow = jnp.exp(cum)
        back = (unit * jnp.exp(-cum)).astype(bf16)
        kn = b["beta"] * (unit * grow)
        ke1 = unit[:C] * jnp.exp(e1 - cum[:C])
        ke2 = unit[C:] * jnp.exp(e2 - cum[C:])
        knb = kn.astype(bf16)
        earlier = jnp.concatenate([ke1.astype(bf16), back[C:]], 0)
        a = jnp.concatenate([mm(knb[:C], back, NT), mm(knb[C:], earlier, NT)], 0)
        b["a"] = jnp.where(i > j, a, 0.0).astype(bf16)
        b["left"] = jnp.concatenate([knb[:C], (kn[C:] * d1).astype(bf16)], 0)
        b["ke"] = jnp.concatenate([(ke1 * d2).astype(bf16), ke2.astype(bf16)], 0)
        b["d"] = d1 * d2
        b["later"] = (grow, d1, back, earlier)
    size = 1
    while size < W:
        mask = ((i // size) % 2 == 1) & ((j // size) == (i // size) - 1)
        odd = range(size, W, 2 * size)
        if size >= 16:
            pick = jnp.concatenate([mask[lo : lo + size] for lo in odd], 0)
            for b in blocks:
                step = jnp.concatenate([b["a"][lo : lo + size] for lo in odd], 0)
                st = mm(jnp.where(pick, step, zero[: W // 2]), b["t"]).astype(bf16)
                full = []
                for n in range(len(odd)):
                    full += [zero[:size], st[n * size : (n + 1) * size]]
                b["st"] = jnp.concatenate(full, 0)
            for b in blocks:
                rows = jnp.concatenate([b["t"][lo : lo + size] for lo in odd], 0)
                rows = rows - mm(rows, b["st"])
                full = []
                for n, lo in enumerate(odd):
                    full += [b["t"][lo - size : lo], rows[n * size : (n + 1) * size]]
                b["t"] = jnp.concatenate(full, 0)
            size *= 2
            continue
        for b in blocks:
            step = jnp.where(mask, b["a"], zero)
            b["st"] = step if size == 1 else mm(step, b["t"]).astype(bf16)
        for b in blocks:
            b["t"] = eye - b["st"].astype(f32) if size == 1 else b["t"] - mm(b["t"], b["st"])
        size *= 2
    for b in blocks:
        right = (b["beta"] * read("v", b).astype(f32)).astype(bf16)
        b["y"] = mm(b["t"], jnp.concatenate([b["left"], right], 1)).astype(bf16)
    for b in blocks:
        b["yk"] = mm(b["y"], b["ke"], TN)
    x = [None] * n_heads
    total = [None] * n_heads
    for p in range(n_blocks):
        for h in range(n_heads):
            b = blocks[h * n_blocks + p]
            if p == 0:
                x[h] = jnp.concatenate([eye * b["d"] - b["yk"][:HS], b["yk"][HS:]], 0)
                total[h] = b["d"]
            else:
                b["x"] = x[h].astype(bf16)
                nx = x[h] * b["d"] - mm(b["x"], b["yk"][:HS])
                x[h] = jnp.concatenate([nx[:HS], nx[HS:] + b["yk"][HS:]], 0)
                total[h] = total[h] * b["d"]
    ends = [(eye * total[h] - x[h][:HS], x[h][HS:], total[h]) for h in range(n_heads)]
    return blocks, ends


def prep_reads(blocks, read, write):
    i, j = masks()
    for b in blocks:
        grow, d1, back, earlier = b["later"]
        qn = read("q", b).astype(f32) * grow
        qnb = qn.astype(bf16)
        r = jnp.concatenate([mm(qnb[:C], back, NT), mm(qnb[C:], earlier, NT)], 0)
        b["r"] = jnp.where(i >= j, r, 0.0).astype(bf16)
        b["qn"] = jnp.concatenate([qn[:C], qn[C:] * d1], 0)
    for b in blocks:
        b["ry"] = mm(b["r"], b["y"])
    for b in blocks:
        qe, local = b["qn"] - b["ry"][:, :HS], b["ry"][:, HS:]
        if "x" in b:
            o = mm(qe, b["x"], NT)
            qe, local = o[:, :HS], o[:, HS:] + local
        write(b, qe.astype(bf16), local)


def kernel(
    q_hbm,
    k_hbm,
    v_hbm,
    ld_hbm,
    wr_hbm,
    gate_hbm,
    gain_hbm,
    w_hbm,
    own_hbm,
    prev_hbm,
    next_hbm,
    q_ref,
    k_ref,
    v_ref,
    ld_ref,
    wr_ref,
    gate_ref,
    gain_ref,
    qd_ref,
    loc_ref,
    msg_ref,
    rmsg,
    pre_map,
    pre_state,
    s_out,
    s_in,
    t_out,
    t_in,
    s0,
    sin_out,
    sin,
    gated,
    qd_sib,
    loc_sib,
    gate_sib,
    sin_sib,
    weights,
    acc,
    psend,
    pvia,
    in_sem,
    m_send,
    m_recv,
    x_send,
    x_recv,
    s_send,
    s_recv,
    l_send,
    l_recv,
    g_send,
    g_recv,
    w_sem,
    w_send,
    w_recv,
    p_send,
    v_recv,
    p_recv,
    o_sem,
):
    outs = (prev_hbm, next_hbm)
    ctx = lax.axis_index("ctx")
    head = lax.axis_index("head")
    x, z = ctx // NZ, ctx % NZ
    y, core = head // NC, head % NC
    feats = qd_ref.shape[2]
    heads = feats // HS
    rows = qd_ref.shape[1] // NY
    sib = (ctx, y * NC + (1 - core))

    def zdev(zz):
        return (x * NZ + zz, head)

    ynext = (ctx, lax.rem(y + 1, NY) * NC + core)
    yprev = (ctx, lax.rem(y + NY - 1, NY) * NC + core)

    def xdev(xx):
        return (xx * NZ + z, head)

    barrier = pltpu.get_barrier_semaphore()
    peers = [zdev(lax.rem(z + s, NZ)) for s in range(1, NZ)] + [ynext, yprev, sib]
    peers += [xdev(lax.rem(x + s, NX)) for s in range(1, NX)]
    loads = []
    for n, (src, dst) in enumerate(
        (
            (ld_hbm, ld_ref),
            (k_hbm, k_ref),
            (wr_hbm, wr_ref),
            (v_hbm, v_ref),
            (q_hbm, q_ref),
            (gate_hbm, gate_ref),
            (gain_hbm, gain_ref),
        )
    ):
        cp = pltpu.make_async_copy(src, dst, in_sem.at[n])
        loads.append(cp)
        if n < 5:
            cp.start()
    wown = pltpu.make_async_copy(w_hbm, weights.at[core], w_sem)
    for peer in peers:
        pl.semaphore_signal(barrier, inc=1, device_id=peer, device_id_type=MESH)

    def remote(src, dst, send, recv, dev):
        return pltpu.make_async_remote_copy(
            src_ref=src, dst_ref=dst, send_sem=send, recv_sem=recv, device_id=dev, device_id_type=MESH
        )

    waited = set()

    def read(name, b):
        for n in dict(ld=(0,), k=(1,), beta=(2,), v=(3,), q=(4,))[name]:
            if n not in waited:
                waited.add(n)
                loads[n].wait()
        at = (slice(b["p"] * W, (b["p"] + 1) * W), slice(b["h"] * HS, (b["h"] + 1) * HS))
        if name == "beta":
            if "beta" not in cache:
                cache["beta"] = wr_ref[...].T
            return cache["beta"][at[0], b["h"] : b["h"] + 1]
        return dict(ld=ld_ref, k=k_ref, v=v_ref, q=q_ref)[name][at]

    cache = {}
    ti = lax.broadcasted_iota(jnp.int32, (MSG - 2 * HS, HS), 0)
    blocks, ends = prep_maps(heads, q_ref.shape[0] // W, read)
    for h, (take, state, total) in enumerate(ends):
        t1 = total.astype(bf16).astype(f32)
        t2 = (total - t1).astype(bf16).astype(f32)
        t3 = total - t1 - t2
        tail = jnp.where(ti == 0, t1, jnp.where(ti == 1, t2, jnp.where(ti == 2, t3, 0.0)))
        msg_ref[h, :HS] = take.astype(bf16)
        msg_ref[h, HS : 2 * HS] = state.astype(bf16)
        msg_ref[h, 2 * HS :] = tail.astype(bf16)

    pl.semaphore_wait(barrier, len(peers))

    sends = []
    for h in range(heads):
        sends.append(remote(msg_ref.at[h], rmsg.at[z], m_send.at[h], m_recv.at[z], zdev(OWNER[h] + core)))

        @pl.when(z != OWNER[h] + core)
        def _(h=h):
            sends[h].start()

        @pl.when(z == OWNER[h] + core)
        def _(h=h):
            rmsg[z] = msg_ref[h]

    wsib = remote(w_hbm, weights.at[core], w_send, w_recv, sib)
    for cp in loads[5:]:
        cp.start()
    wown.start()

    owner = z % 2 == core
    slot = (z // 4) + 2 * ((z // 2) % 2)

    def write(b, qd, local):
        cols = slice(b["h"] * HS, (b["h"] + 1) * HS)
        lo = b["p"] * W
        while lo < (b["p"] + 1) * W:
            jj = lo // rows
            hi = min((b["p"] + 1) * W, (jj + 1) * rows)
            to = (jj // NC) * rows + lo - jj * rows
            qd_ref[jj % NC, to : to + hi - lo, cols] = qd[lo - b["p"] * W : hi - b["p"] * W]
            loc_ref[jj % NC, to : to + hi - lo, cols] = local[lo - b["p"] * W : hi - b["p"] * W]
            lo = hi

    prep_reads(blocks, read, write)
    lent = [
        remote(qd_ref.at[1 - core], qd_sib, l_send.at[0], l_recv.at[0], sib),
        remote(loc_ref.at[1 - core], loc_sib, l_send.at[1], l_recv.at[1], sib),
        remote(gate_hbm.at[:, 1 - core], gate_sib, l_send.at[2], l_recv.at[2], sib),
    ]
    for cp in lent:
        cp.start()
    wsib.start()
    for n in (5, 6):
        loads[n].wait()
    states = [remote(s_out, s_in, x_send.at[xx - 1], x_recv.at[0], xdev(xx)) for xx in (3, 2, 1)]
    totals1 = [remote(t_out, t_in.at[0], x_send.at[xx - 1], x_recv.at[1], xdev(xx)) for xx in (3, 2)]
    totals2 = [remote(t_out, t_in.at[1], x_send.at[xx - 1], x_recv.at[2], xdev(xx)) for xx in (3,)]
    backs = []
    for s in (4, 3, 5, 2, 6, 1, 7):
        zz = lax.rem(z + s, NZ)
        backs.append((zz, remote(sin_out.at[zz], sin.at[slot], s_send.at[s], s_recv.at[slot], zdev(zz))))

    @pl.when(owner)
    def _():
        ei = lax.broadcasted_iota(jnp.int32, (2 * HS, HS), 0)
        ej = lax.broadcasted_iota(jnp.int32, (2 * HS, HS), 1)
        run = (ei == ej).astype(f32)
        for zz in range(NZ):

            @pl.when(z != zz)
            def _(zz=zz):
                remote(msg_ref.at[0], rmsg.at[zz], m_send.at[0], m_recv.at[zz], zdev(zz)).wait_recv()

            pre_map[zz] = run[:HS].astype(bf16)
            pre_state[zz] = run[HS:]
            d = jnp.sum(rmsg[zz, 2 * HS :, :].astype(f32), axis=0, keepdims=True)
            new = run * d - mm(run, rmsg[zz, :HS, :])
            run = jnp.concatenate([new[:HS], new[HS:] + rmsg[zz, HS : 2 * HS, :].astype(f32)], 0)

        @pl.when(x == 0)
        def _():
            s_out[...] = run[HS:].astype(bf16)
            for cp in states:
                cp.start()
            s0[...] = jnp.zeros_like(s0)

        @pl.when((x == 1) | (x == 2))
        def _():
            t_out[...] = run.astype(bf16)

        @pl.when(x == 1)
        def _():
            for cp in totals1:
                cp.start()
            states[0].wait_recv()
            s0[...] = s_in[...]

        @pl.when(x == 2)
        def _():
            totals2[0].start()

        @pl.when(x >= 2)
        def _():
            states[0].wait_recv()
            totals1[0].wait_recv()
            s0[...] = (mm(s_in[...], t_in[0, :HS]) + t_in[0, HS:].astype(f32)).astype(bf16)

        @pl.when(x == 3)
        def _():
            totals2[0].wait_recv()
            s0[...] = (mm(s0[...], t_in[1, :HS]) + t_in[1, HS:].astype(f32)).astype(bf16)

        s0v = s0[...]
        for zz in range(NZ):
            sin_out[zz] = (mm(s0v, pre_map[zz]) + pre_state[zz]).astype(bf16)
        for zz, cp in backs:
            cp.start()
        sin[slot] = sin_out[z]

    def gate_of(att, gate):
        ms = jnp.mean(att * att, axis=-1, keepdims=True)
        gate = jax.nn.sigmoid(gate.astype(f32).reshape(NY * rows, HS))
        return (att * lax.rsqrt(ms + 1e-5) * gain_ref[...] * gate).astype(bf16)

    passed = []
    for h in range(heads):

        @pl.when(z != OWNER[h] + core)
        def _(h=h):
            remote(sin_out.at[0], sin.at[h], s_send.at[0], s_recv.at[h], zdev(OWNER[h] + core)).wait_recv()

        cp = remote(sin.at[h], sin_sib.at[h], g_send.at[h], g_recv.at[h], sib)
        cp.start()
        passed.append(cp)
    for h in range(heads):
        cols = slice(h * HS, (h + 1) * HS)
        att = mm(qd_ref[core, :, cols], sin[h], NT) + loc_ref[core, :, cols]
        gated[0, :, cols] = gate_of(att, gate_ref[:, core, :, cols])

    started = []
    tile = weights.shape[2] // NT_OUT
    wide = 2 * tile
    wown.wait()
    mine = gated[0]
    for t in range(NT_OUT // 2):
        acc[t] = mm(mine, weights[core, :, t * wide : (t + 1) * wide])
    for cp in lent + passed:
        cp.wait()
    for h in range(heads):
        cols = slice(h * HS, (h + 1) * HS)
        att = mm(qd_sib[:, cols], sin_sib[h], NT) + loc_sib[:, cols]
        gated[1, :, cols] = gate_of(att, gate_sib[:, :, cols])
    wsib.wait()
    other = gated[1]
    y1, y2, y3 = [lax.rem(y + s, NY) for s in range(1, NY)]
    for t in range(NT_OUT // 2):
        val = acc[t] + mm(other, weights[1 - core, :, t * wide : (t + 1) * wide])
        val = val.reshape(NY, rows, wide).astype(bf16)
        for u in range(2):
            psend[2 * t + u] = val[:, :, u * tile : (u + 1) * tile]
        for u in range(2):
            n = 2 * t + u
            cp = remote(psend.at[n, y2], pvia.at[n], p_send.at[0, n], v_recv.at[n], (ynext, yprev)[u])
            cp.start()
            started.append(cp)
    for t in range(NT_OUT):
        u = t % 2
        cp = remote(
            psend.at[t, (y3, y1)[u]],
            outs[1 - u].at[:, t * tile : (t + 1) * tile],
            p_send.at[1, t],
            p_recv.at[1 - u, t],
            (yprev, ynext)[u],
        )
        cp.start()
        started.append(cp)
    locals_ = []
    for t in range(NT_OUT):
        cp = pltpu.make_async_copy(psend.at[t, y], own_hbm.at[:, t * tile : (t + 1) * tile], o_sem.at[t])
        cp.start()
        locals_.append(cp)
    for t in range(NT_OUT // 2):
        for u in range(2):
            n = 2 * t + u
            remote(
                psend.at[n, 0], pvia.at[n], p_send.at[0, n], v_recv.at[n], (yprev, ynext)[u]
            ).wait_recv()
        for u in range(2):
            n = 2 * t + u
            near = (y1, y3)[u]
            psend[n, near] = (psend[n, near].astype(f32) + pvia[n].astype(f32)).astype(bf16)
        for u in range(2):
            n = 2 * t + u
            cp = remote(
                psend.at[n, (y1, y3)[u]],
                outs[u].at[:, n * tile : (n + 1) * tile],
                p_send.at[2, n],
                p_recv.at[u, n],
                (ynext, yprev)[u],
            )
            cp.start()
            started.append(cp)
    for t in range(NT_OUT):
        for side in range(2):
            cols = slice(t * tile, (t + 1) * tile)
            remote(
                psend.at[t, 0], outs[side].at[:, cols], p_send.at[0, t], p_recv.at[side, t], (yprev, ynext)[side]
            ).wait_recv()
    for cp in locals_:
        cp.wait()

    for h in range(heads):

        @pl.when(z != OWNER[h] + core)
        def _(h=h):
            sends[h].wait_send()

    @pl.when(owner)
    def _():
        for _, cp in backs:
            cp.wait_send()

    for xx, copies in enumerate((states, totals1, totals2)):

        @pl.when(owner & (x == xx))
        def _(copies=copies):
            for cp in copies:
                cp.wait_send()

    for cp in started:
        cp.wait_send()


def on_device(q, k, v, ld, wr, gate, gain, w):
    toks, feats = q.shape
    heads = feats // HS
    kd, width = w.shape
    rb = toks // (NY * NC)
    tile = width // NT_OUT
    anyspec = pl.BlockSpec(memory_space=pltpu.HBM)
    vmem, dma = pltpu.VMEM, pltpu.SemaphoreType.DMA
    out = jax.ShapeDtypeStruct((rb, width), bf16)
    own, one, two = pl.pallas_call(
        kernel,
        in_specs=[anyspec] * 8,
        out_specs=[pl.BlockSpec(memory_space=pltpu.VMEM)] * 3,
        out_shape=[out] * 3,
        scratch_shapes=[
            vmem((toks, feats), bf16),
            vmem((toks, feats), bf16),
            vmem((toks, feats), bf16),
            vmem((toks, feats), f32),
            vmem((heads, toks), f32),
            vmem((NY, NC, rb, feats), bf16),
            vmem((1, HS), f32),
            vmem((NC, NY * rb, feats), bf16),
            vmem((NC, NY * rb, feats), f32),
            vmem((heads, MSG, HS), bf16),
            vmem((NZ, MSG, HS), bf16),
            vmem((NZ, HS, HS), bf16),
            vmem((NZ, HS, HS), f32),
            vmem((HS, HS), bf16),
            vmem((HS, HS), bf16),
            vmem((2 * HS, HS), bf16),
            vmem((2, 2 * HS, HS), bf16),
            vmem((HS, HS), bf16),
            vmem((NZ, HS, HS), bf16),
            vmem((heads, HS, HS), bf16),
            vmem((NC, NY * rb, kd), bf16),
            vmem((NY * rb, kd), bf16),
            vmem((NY * rb, kd), f32),
            vmem((NY, rb, kd), bf16),
            vmem((heads, HS, HS), bf16),
            vmem((NC, kd, width), bf16),
            vmem((NT_OUT // 2, NY * rb, 2 * tile), f32),
            vmem((NT_OUT, NY, rb, tile), bf16),
            vmem((NT_OUT, rb, tile), bf16),
            dma((7,)),
            dma((heads,)),
            dma((NZ,)),
            dma((3,)),
            dma((3,)),
            dma((NZ,)),
            dma((heads,)),
            dma((3,)),
            dma((3,)),
            dma((heads,)),
            dma((heads,)),
            dma,
            dma,
            dma,
            dma((3, NT_OUT)),
            dma((NT_OUT,)),
            dma((2, NT_OUT)),
            dma((NT_OUT,)),
        ],
        compiler_params=pltpu.CompilerParams(
            collective_id=0, has_side_effects=True, vmem_limit_bytes=40 << 20
        ),
        name="delta_layer",
    )(*[pltpu.with_memory_space_constraint(a, pltpu.HBM) for a in (q, k, v, ld, wr.T, gate.reshape(NY, NC, rb, feats), gain.reshape(1, HS), w)])
    return (own.astype(f32) + one.astype(f32) + two.astype(f32)).astype(bf16)


def solution(mesh):
    in_specs = (
        P("ctx", "head"),
        P("ctx", "head"),
        P("ctx", "head"),
        P("ctx", "head"),
        P("ctx", "head"),
        P("ctx", "head"),
        P(),
        P("head", None),
    )
    out_specs = P(("ctx", "head"), None)
    return jax.shard_map(
        on_device, mesh=mesh, in_specs=in_specs, out_specs=out_specs, check_vma=False
    )
```
